128 devices in a mesh: dp: 2 (over core), seq: 16 (over y, x), tensor: 4 (over z).
Axes of the slice: x: 4, y: 4, z: 4, core: 2. Of those that a mesh axis runs over, the one named last changes fastest.
Arguments:
- pool: bfloat16 [2048, 16, 1792], P(('dp', 'seq'), 'tensor')
- page_table: int32 [8, 256], replicated, may hold values from 0 to 2047, as said below
- reassign: int32 [8], replicated, may hold values from 0 to 7, as said below
- lengths: int32 [8], replicated, may hold values from 1 to 4096, as said below
- gain_one: float32 [1792], replicated, may hold values from 0.1 to 1.9
- w_featmap: bfloat16 [1792, 2, 256], P(None, None, 'tensor'), may hold values from -0.25 to 0.25
- w_value: bfloat16 [1792, 1792], P(None, 'tensor'), may hold values from -0.125 to 0.125
- w_out_one: bfloat16 [1792, 1792], P('tensor'), may hold values from -0.5 to 0.5
- gain_two: float32 [1792], replicated, may hold values from 0.1 to 1.9
- w_window: bfloat16 [1792, 3, 1792], P(None, None, 'tensor')
- conv_window: float32 [3, 3, 1792], P(None, None, 'tensor')
- w_out_two: bfloat16 [1792, 1792], P('tensor'), may hold values from -0.125 to 0.125
Outputs:
- out: bfloat16 [8, 256, 16, 1792], P('dp', 'seq', 'tensor')
The draws below stay inside these ranges and needn't reach their ends.
Inputs may be any that keep to these rules, and one draw needn't show every extreme that they name: A permutation: output slot i holds request reassign[i]; requests are dealt by falling length to the 2 groups of 4 slots in alternating order, so the first slot of every group holds a request of length 4096. page_table[r, p] is the pool page that holds positions p * 16 to p * 16 + 15 of request r, and every pool page is named once. Take the pool in aligned blocks of 64 pages, and the pages that the output needs in blocks: block g * 16 + b holds positions b * 256 to b * 256 + 255 of slots g * 4 to g * 4 + 3. No pool block holds more than 2 pages of one such block, and 2 is reached. `lengths`: at least 2 requests have length 4096.
All inputs are finite; a program needn't handle non-finite values.
Results may differ from the reference program's by a relative error of at most 0.039.
Values may be sent and summed in bfloat16 or wider, within the bound.
A program may use at most 256 MiB of HBM per device.

```python
import jax
import jax.numpy as jnp
from jax import lax

D = 1792
HEADS = 16
HEAD = 112
FEAT = 16
WINDOW = 64
KERNEL = 3
PAGE = 16
REQ_DEV = 4
BLOCK = 256
FEATS = 256
LEN = 4096
PAGES = 256
PAGES_DEV = 64
REQUESTS = 8
POOL_PAGES = 2048
N_DP = 2
N_SEQ = 16
N_TENSOR = 4


def routing_tables(key):
    base_key = jax.random.fold_in(key, 11)
    group_key, slot_key, length_key, long_key, tie_key = jax.random.split(base_key, 5)
    devices_all = N_DP * N_SEQ
    block_pages = BLOCK // PAGE
    raw_lengths = jax.random.randint(length_key, (REQUESTS,), 1, LEN + 1, jnp.int32)
    long_pick = jax.random.permutation(long_key, REQUESTS) < N_DP
    lengths = jnp.where(long_pick, LEN, raw_lengths).astype(jnp.int32)
    ties = jax.random.permutation(tie_key, REQUESTS).astype(jnp.int32)
    score = lengths * REQUESTS + ties
    order = jnp.argsort(-score).astype(jnp.int32)
    rank = jnp.arange(REQUESTS, dtype=jnp.int32)
    rounds = rank // N_DP
    within = rank % N_DP
    group = jnp.where(rounds % 2 == 0, within, N_DP - 1 - within)
    slot = group * REQ_DEV + rounds
    reassign = jnp.zeros((REQUESTS,), jnp.int32).at[slot].set(order)
    device_order = jax.random.permutation(group_key, devices_all).astype(jnp.int32)
    slot_keys = jax.random.split(slot_key, devices_all)
    slot_orders = jax.vmap(lambda one_key: jax.random.permutation(one_key, PAGES_DEV))(slot_keys).astype(jnp.int32)
    target = jnp.arange(devices_all, dtype=jnp.int32)[:, None]
    local_page = jnp.arange(PAGES_DEV, dtype=jnp.int32)[None, :]
    source = device_order[(target + local_page) % devices_all]
    pool_index = source * PAGES_DEV + slot_orders[source, jnp.broadcast_to(local_page, source.shape)]
    inverse = jnp.argsort(reassign).astype(jnp.int32)
    request_ids = jnp.arange(REQUESTS, dtype=jnp.int32)[:, None]
    page_ids = jnp.arange(PAGES, dtype=jnp.int32)[None, :]
    slot_ids = inverse[request_ids]
    target_ids = slot_ids // REQ_DEV * N_SEQ + page_ids // block_pages
    local_ids = slot_ids % REQ_DEV * block_pages + page_ids % block_pages
    page_table = pool_index[target_ids, local_ids]
    return (reassign, page_table.astype(jnp.int32), lengths)


def draw_reassign(key, part):
    return routing_tables(key)[0]


def draw_page_table(key, part):
    return routing_tables(key)[1]


def draw_lengths(key, part):
    return routing_tables(key)[2]


def draw_pool(key, part):
    first_key = jax.random.fold_in(key, 0)
    draws = jax.random.normal(first_key, (POOL_PAGES, PAGE, D), jnp.float32)
    return draws.astype(jnp.bfloat16)


def draw_w_window(key, part):
    first_key = jax.random.fold_in(key, 0)
    spread = D ** (-0.5)
    draws = jax.random.normal(first_key, (D, 3, D), jnp.float32) * spread
    return draws.astype(jnp.bfloat16)


def draw_conv_window(key, part):
    first_key, second_key = jax.random.split(key, 2)
    leading = jax.random.uniform(first_key, (1, 3, D), jnp.float32, 0.6, 1.4)
    others = 0.3 * jax.random.normal(second_key, (KERNEL - 1, 3, D), jnp.float32)
    return jnp.concatenate([leading, others], axis=0)


def steps_of(own_key, shape, pieces, low, high):
    def one(axis_at, blocks):
        heights = jax.random.uniform(jax.random.fold_in(jax.random.fold_in(own_key, 6), axis_at), (blocks,), jnp.float32, low / len(pieces), high / len(pieces))
        return jnp.repeat(jnp.exp(heights), shape[axis_at] // blocks).reshape((-1,) + (1,) * (len(shape) - axis_at - 1))

    gain = one(*pieces[0])
    for cut in pieces[1:]:
        gain = gain * one(*cut)
    return gain


def gaussian(key, extent, width, bound, shards=(), kind=jnp.bfloat16):
    array = width * jax.random.normal(key, extent, jnp.float32)
    if shards:
        array = array * steps_of(key, extent, shards, -0.22, 0.18)
    return jnp.clip(array, -bound, bound).astype(kind)


def setup_inputs(seed: int = 0) -> dict:
    splits = jax.random.split(jax.random.key(seed), 13)
    pool = draw_pool(jax.random.fold_in(splits[12], 71), 0)
    page_table = draw_page_table(jax.random.fold_in(splits[12], 71), 0)
    reassign = draw_reassign(jax.random.fold_in(splits[12], 71), 0)
    lengths = draw_lengths(jax.random.fold_in(splits[12], 71), 0)
    gain_one = jnp.clip(1.0 + 0.18 * jax.random.normal(splits[4], (D,), jnp.float32), 0.1, 1.9)
    w_featmap = gaussian(splits[5], (D, 2, FEATS), (D // 4) ** -0.5, 0.25, ((2, 4),))
    w_value = gaussian(splits[6], (D, D), D ** -0.5, 0.125, ((1, 4),))
    w_out_one = gaussian(splits[7], (D, D), (D // 16) ** -0.5, 0.5, ((0, 4),))
    gain_two = jnp.clip(1.0 + 0.18 * jax.random.normal(splits[8], (D,), jnp.float32), 0.1, 1.9)
    w_window = draw_w_window(jax.random.fold_in(splits[12], 71), 0)
    conv_window = draw_conv_window(jax.random.fold_in(splits[12], 71), 0)
    w_out_two = gaussian(splits[11], (D, D), D ** -0.5, 0.125, ((0, 4),))
    return {"pool": pool, "page_table": page_table, "reassign": reassign, "lengths": lengths, "gain_one": gain_one, "w_featmap": w_featmap, "w_value": w_value, "w_out_one": w_out_one, "gain_two": gain_two, "w_window": w_window, "conv_window": conv_window, "w_out_two": w_out_two}


norm_eps = 1e-05

def rounded(values):
    return lax.optimization_barrier(values.astype(jnp.bfloat16)).astype(jnp.float32)

def rms_normed(row_block, gain_vector):
    values = row_block.astype(jnp.float32)
    scale = lax.rsqrt(lax.optimization_barrier(jnp.mean(values * values, axis=-1, keepdims=True)) + norm_eps)
    return (values * scale * gain_vector).astype(jnp.bfloat16)

def causal_conv(projected, tap_table):
    seq_rows = projected.shape[0]
    padded = jnp.pad(projected, ((KERNEL - 1, 0), (0, 0)))
    total = tap_table[0] * padded[KERNEL - 1:KERNEL - 1 + seq_rows]
    for offset in range(1, KERNEL):
        total = total + tap_table[offset] * padded[KERNEL - 1 - offset:KERNEL - 1 - offset + seq_rows]
    return total

def grouped_sum(mixed, weight):
    group_cols = D // N_TENSOR
    total = jnp.zeros((mixed.shape[0], D), jnp.float32)
    for group in range(N_TENSOR):
        partial_value = jnp.dot(mixed[:, group * group_cols:(group + 1) * group_cols], weight[group * group_cols:(group + 1) * group_cols], preferred_element_type=jnp.float32)
        total = total + rounded(partial_value)
    return total

def reference(pool, page_table, reassign, lengths, gain_one, w_featmap, w_value, w_out_one, gain_two, w_window, conv_window, w_out_two):
    highest = lax.Precision.HIGHEST

    def one_request(carried):
        tokens, prompt_length = carried
        normed_one = rms_normed(tokens, gain_one)
        featured = jnp.dot(normed_one, w_featmap.reshape(D, 2 * FEATS), preferred_element_type=jnp.float32)
        queries = rounded(featured[:, :FEATS]).reshape(LEN, HEADS, FEAT)
        key_rows = rounded(featured[:, FEATS:]).reshape(LEN, HEADS, FEAT)
        values = rounded(jnp.dot(normed_one, w_value, preferred_element_type=jnp.float32)).reshape(LEN, HEADS, HEAD)
        scores = jnp.einsum('thf,uhf->htu', queries, key_rows, precision=highest) * FEAT ** (-0.5)
        causal = jnp.arange(LEN)[None, :] <= jnp.arange(LEN)[:, None]
        kernel = jnp.where(causal[None], 1.0 + scores + 0.5 * scores * scores, 0.0)
        numerator = jnp.einsum('htu,uhd->thd', kernel, values, precision=highest)
        denominator = lax.optimization_barrier(jnp.sum(kernel, axis=2)).T
        mixed_one = (numerator / denominator[..., None]).reshape(LEN, D).astype(jnp.bfloat16)
        residual_one = (tokens.astype(jnp.float32) + grouped_sum(mixed_one, w_out_one)).astype(jnp.bfloat16)
        normed_two = rms_normed(residual_one, gain_two)
        projected = jnp.dot(normed_two, w_window.reshape(D, 3 * D), preferred_element_type=jnp.float32)
        convolved = rounded(causal_conv(projected, conv_window.reshape(KERNEL, 3 * D)))
        queries_two = convolved[:, :D].reshape(LEN, HEADS, HEAD)
        keys_two = convolved[:, D:2 * D].reshape(LEN, HEADS, HEAD)
        values_two = convolved[:, 2 * D:].reshape(LEN, HEADS, HEAD)
        logits = jnp.einsum('thd,uhd->htu', queries_two, keys_two, precision=highest) * HEAD ** (-0.5)
        query_pos = jnp.arange(LEN)[:, None]
        key_pos = jnp.arange(LEN)[None, :]
        allowed = (key_pos <= query_pos) & (key_pos > query_pos - WINDOW)
        logits = jnp.where(allowed[None], logits, -jnp.inf)
        row_top = lax.optimization_barrier(jnp.max(logits, axis=2, keepdims=True))
        weights = jnp.exp(logits - row_top)
        attention = rounded(weights / lax.optimization_barrier(jnp.sum(weights, axis=2, keepdims=True)))
        mixed_two = jnp.einsum('htu,uhd->thd', attention, values_two, precision=highest).reshape(LEN, D).astype(jnp.bfloat16)
        result = (residual_one.astype(jnp.float32) + grouped_sum(mixed_two, w_out_two)).astype(jnp.bfloat16)
        positions = jnp.arange(LEN)
        result = jnp.where((positions < prompt_length)[:, None], result, jnp.zeros_like(result))
        return result.reshape(PAGES, PAGE, D)
    tokens = pool[page_table[reassign]].reshape(REQUESTS, LEN, D)
    prompt_length = lengths[reassign]
    return lax.map(one_request, (tokens, prompt_length))
```

```python
import functools

import jax
import jax.numpy as jnp
from jax import lax
from jax.experimental import pallas as pl
from jax.experimental.pallas import tpu as pltpu
from jax.sharding import PartitionSpec as P

HEAD = 112
FEAT = 16
WINDOW = 64
D = 1792
ROWS = 256
HALO = 80
QUARTERS = 4
QHEADS = 4
STATE = 176
NORM_EPS = 1e-05
MESH = pl.DeviceIdType.MESH
BF = jnp.bfloat16
F32 = jnp.float32
ANY = pl.BlockSpec(memory_space=pl.ANY)
VM = pl.BlockSpec(memory_space=pltpu.VMEM)


def dot(a, b, dims=((1,), (0,))):
    return lax.dot_general(a, b, (dims, ((), ())), preferred_element_type=F32)


def places():
    core, seq, z = lax.axis_index("dp"), lax.axis_index("seq"), lax.axis_index("tensor")
    return core, seq, z, seq // 4, seq % 4


def piece(ref, kind, shape, core, q, half=None):
    rows, cols = shape
    count = rows // 8 if kind == "r" else rows // 4
    start = q * count + (core * (rows // 2) if kind == "r" else 0)
    if half is not None:
        count //= 2
        start = start + half * count
    row_part = pl.ds(pl.multiple_of(start, 8), count)
    if kind == "r":
        return ref.at[row_part, :]
    return ref.at[row_part, pl.ds(pl.multiple_of(core * (cols // 2), 128), cols // 2)]


def gather_kernel(kinds, *refs):
    n = len(kinds)
    ins, taps, outs, taps_out = refs[:n], refs[n], refs[n + 1 : 2 * n + 1], refs[2 * n + 1]
    send_sems, recv_sems = refs[2 * n + 2 :]
    core, seq, z, y, x = places()
    p = jnp.where(core == 0, x, y)

    def at(k):
        q = (p + k) % 4
        return (core, jnp.where(core == 0, y * 4 + q, q * 4 + x), z)

    up, down, far = (core, seq, (z + 1) % 4), (core, seq, (z + 3) % 4), (core, seq, (z + 2) % 4)
    right, left, other = at(1), at(3), (1 - core, seq, z)
    barrier = pltpu.get_barrier_semaphore()
    for peer in (up, down, far, right, left, other):
        pl.semaphore_signal(barrier, inc=1, device_id=peer, device_id_type=MESH)
    pl.semaphore_wait(barrier, 6)
    sends = []

    def send(src, dst, peer):
        k = len(sends)
        copy = pltpu.make_async_remote_copy(
            src_ref=src,
            dst_ref=dst,
            send_sem=send_sems.at[k],
            recv_sem=recv_sems.at[k],
            device_id=peer,
            device_id_type=MESH,
        )
        copy.start()
        sends.append(copy)
        return copy

    def view(i, ref, q, half=None):
        return piece(ref, *kinds[i], core, q, half)

    def along(i, d, q, half, peer):
        part = view(i, outs[i].at[d], q, half)
        return send(part, part, peer)

    first = []
    for i in range(n):
        mine = view(i, ins[i], p)
        first.append(
            (send(mine, view(i, outs[i].at[0], p), down), send(mine, view(i, outs[i].at[2], p), up))
        )
    small = [send(taps, taps_out.at[k], peer) for k, peer in ((0, down), (1, far), (2, up))]
    last = []
    ring = {}
    ends = {}

    def start_ring(i):
        from_up, from_down = first[i]
        from_up.wait_recv()
        low = send(view(i, outs[i].at[0], p, 0), view(i, outs[i].at[1], p, 0), down)
        ring[i, 0] = (along(i, 0, p, None, right), along(i, 0, p, None, left))
        from_down.wait_recv()
        high = send(view(i, outs[i].at[2], p, 1), view(i, outs[i].at[1], p, 1), up)
        ring[i, 2] = (along(i, 2, p, None, right), along(i, 2, p, None, left))
        last.append(along(i, 0, p, None, other))
        last.append(along(i, 2, p, None, other))
        low.wait_recv()
        high.wait_recv()
        ring[i, 1] = (along(i, 1, p, None, right), along(i, 1, p, None, left))
        last.append(along(i, 1, p, None, other))

    def pass_on(i):
        for d in (0, 2, 1):
            from_left, from_right = ring[i, d]
            from_left.wait_recv()
            a = along(i, d, (p + 3) % 4, 0, right)
            last.append(along(i, d, (p + 3) % 4, None, other))
            from_right.wait_recv()
            b = along(i, d, (p + 1) % 4, 1, left)
            last.append(along(i, d, (p + 1) % 4, None, other))
            ends[i, d] = (a, b)

    def finish(i):
        for d in (0, 2, 1):
            for copy in ends[i, d]:
                copy.wait_recv()
            last.append(along(i, d, (p + 2) % 4, None, other))

    for i in range(n):
        start_ring(i)
        if i >= 1:
            pass_on(i - 1)
        if i >= 2:
            finish(i - 2)
    pass_on(n - 1)
    finish(n - 2)
    finish(n - 1)
    for copy in small + last:
        copy.wait_recv()
    for copy in sends:
        copy.wait_send()


def gather_weights(kinds, arrays, taps):
    n = len(kinds)
    copies = 28 * n + 3
    return pl.pallas_call(
        functools.partial(gather_kernel, kinds),
        out_shape=[jax.ShapeDtypeStruct((3,) + a.shape, a.dtype) for a in arrays + [taps]],
        in_specs=[ANY] * (n + 1),
        out_specs=[ANY] * (n + 1),
        scratch_shapes=[pltpu.SemaphoreType.DMA((copies,)), pltpu.SemaphoreType.DMA((copies,))],
        compiler_params=pltpu.CompilerParams(collective_id=0, has_side_effects=True),
        name="gather_weights",
    )(*arrays, taps)


def position_of(sigma):
    return sigma % 64 // 4 * 16 + sigma // 64 * 4 + sigma % 4


def row_order(to_positions):
    a = lax.broadcasted_iota(jnp.int32, (ROWS, ROWS), 0)
    b = lax.broadcasted_iota(jnp.int32, (ROWS, ROWS), 1)
    hit = (position_of(b) == a) if to_positions else (position_of(a) == b)
    return hit.astype(F32).astype(BF)


def normed(values, gain):
    wide = values.astype(F32)
    scale = lax.rsqrt(jnp.mean(wide * wide, axis=-1, keepdims=True) + NORM_EPS)
    return (wide * scale * gain).astype(BF)


def build_spread(spread):
    r = lax.broadcasted_iota(jnp.int32, (128, 256), 0)
    f = lax.broadcasted_iota(jnp.int32, (128, 256), 1)
    i, j = f % 16, (f + f // 16) % 16
    for h in range(QHEADS):
        for side in range(2):
            base = side * 64 + h * 16
            one = (r == base + i) & (f < 160)
            two = (r == base + j) & (f < 144)
            spread[h, side, 0] = one.astype(F32).astype(BF)
            spread[h, side, 1] = two.astype(F32).astype(BF)


def spread_pair(rows, spread, h, side):
    f = lax.broadcasted_iota(jnp.int32, (1, 256), 1)
    one = dot(rows, spread[h, side, 0]) + (f == 160).astype(F32)
    two = dot(rows, spread[h, side, 1]) + ((f >= 144) & (f <= 160)).astype(F32)
    return one * two


def key_weights():
    f = lax.broadcasted_iota(jnp.int32, (1, 256), 1)
    pair = jnp.where((f < 16) | (f >= 128), 1.0 / 32, 1.0 / 16)
    return jnp.where(f < 144, pair, jnp.where(f < 160, 0.25, 1.0)).astype(F32)


def local_layer_one(d, x_normed, weight, spread, nd, phi, state):
    projected = dot(x_normed, weight).astype(BF)
    both = projected[:, :128]
    queries, keys = projected[:, :64], projected[:, 64:128]
    lane = lax.broadcasted_iota(jnp.int32, (ROWS, 64), 1)
    a = lax.broadcasted_iota(jnp.int32, (ROWS, ROWS), 0)
    b = lax.broadcasted_iota(jnp.int32, (ROWS, ROWS), 1)
    ones = (lax.broadcasted_iota(jnp.int32, (ROWS, 128), 1) == HEAD).astype(F32).astype(BF)
    for h in range(QHEADS):
        head = d * QHEADS + h
        mine = jnp.where(lane // 16 == h, queries, jnp.zeros_like(queries))
        s = dot(mine, keys, ((1,), (1,))) * 0.25
        kernel = jnp.where(b <= a, 1.0 + s + 0.5 * s * s, 0.0).astype(BF)
        values = projected[:, 128 * (h + 1) : 128 * (h + 2)] + ones
        nd[head] = dot(kernel, values)
        phi[head] = spread_pair(both, spread, h, 0).astype(BF)
        key_phi = (spread_pair(both, spread, h, 1) * key_weights()).astype(BF)
        state[head] = dot(key_phi, values, ((0,), (0,)))[:STATE].astype(BF)


def layer_one_local_kernel(
    arrived, gain, own, others, x_out, nd, phi, state, weights, spread, xn, sems
):
    copies = [pltpu.make_async_copy(own, weights.at[0], sems.at[0])] + [
        pltpu.make_async_copy(others.at[k], weights.at[k + 1], sems.at[k + 1]) for k in range(3)
    ]
    for copy in copies:
        copy.start()
    build_spread(spread)
    x = dot(row_order(True), arrived[...].reshape(ROWS, D)).astype(BF)
    x_out[...] = x
    xn[...] = normed(x, gain[...])
    for d in range(QUARTERS):
        copies[d].wait()
        local_layer_one(d, xn[...], weights[d], spread, nd, phi, state)


def layer_one_local(arrived, gain, own, others):
    heads = QUARTERS * QHEADS
    return pl.pallas_call(
        layer_one_local_kernel,
        out_shape=[
            jax.ShapeDtypeStruct((ROWS, D), BF),
            jax.ShapeDtypeStruct((heads, ROWS, 128), F32),
            jax.ShapeDtypeStruct((heads, ROWS, 256), BF),
            jax.ShapeDtypeStruct((heads, STATE, 128), BF),
        ],
        in_specs=[VM, VM, ANY, ANY],
        out_specs=[VM] * 4,
        scratch_shapes=[
            pltpu.VMEM((QUARTERS, D, 640), BF),
            pltpu.VMEM((QHEADS, 2, 2, 128, 256), BF),
            pltpu.VMEM((ROWS, D), BF),
            pltpu.SemaphoreType.DMA((QUARTERS,)),
        ],
        compiler_params=pltpu.CompilerParams(vmem_limit_bytes=48 << 20),
        name="layer_one_local",
    )(arrived, gain, own, others)


def pack_heads():
    a = lax.broadcasted_iota(jnp.int32, (512, 448), 0)
    b = lax.broadcasted_iota(jnp.int32, (512, 448), 1)
    hit = (a // 128 == b // HEAD) & (a % 128 == b % HEAD)
    return hit.astype(F32).astype(BF)


def unpack_heads():
    a = lax.broadcasted_iota(jnp.int32, (448, 512), 0)
    b = lax.broadcasted_iota(jnp.int32, (448, 512), 1)
    hit = (b // 128 == a // HEAD) & (b % 128 == a % HEAD)
    return hit.astype(F32).astype(BF)


def layer_one_mix_kernel(x, nd, phi, prior, own, others, out, weights, total, wide, sems):
    copies = [pltpu.make_async_copy(own, weights.at[0], sems.at[0])] + [
        pltpu.make_async_copy(others.at[k], weights.at[k + 1], sems.at[k + 1]) for k in range(3)
    ]
    for copy in copies:
        copy.start()
    pack = pack_heads()
    for d in range(QUARTERS):
        for h in range(QHEADS):
            head = d * QHEADS + h
            both = nd[head] + dot(phi[head][:, :STATE], prior[head])
            mixed = both / both[:, HEAD : HEAD + 1]
            wide[:, 128 * h : 128 * (h + 1)] = mixed.astype(BF)
        mixed = dot(wide[...], pack).astype(BF)
        copies[d].wait()
        part = dot(mixed, weights[d]).astype(BF).astype(F32)
        total[...] = part if d == 0 else total[...] + part
    out[...] = (x[...].astype(F32) + total[...]).astype(BF)


def layer_one_mix(x, nd, phi, prior, own, others):
    return pl.pallas_call(
        layer_one_mix_kernel,
        out_shape=jax.ShapeDtypeStruct((ROWS, D), BF),
        in_specs=[VM] * 4 + [ANY] * 2,
        out_specs=VM,
        scratch_shapes=[
            pltpu.VMEM((QUARTERS, 448, D), BF),
            pltpu.VMEM((ROWS, D), F32),
            pltpu.VMEM((ROWS, 512), BF),
            pltpu.SemaphoreType.DMA((QUARTERS,)),
        ],
        compiler_params=pltpu.CompilerParams(vmem_limit_bytes=48 << 20),
        name="layer_one_mix",
    )(x, nd, phi, prior, own, others)


def layer_two_quarter(first_block, xn, weight, taps, unpack, qkv, wide):
    span = ROWS + WINDOW
    for part in range(3):
        cols = slice(448 * part, 448 * (part + 1))
        projected = dot(xn, weight[:, cols])
        conv = taps[part : part + 1] * projected[HALO - WINDOW :]
        for j in (1, 2):
            row = 3 * j + part
            conv = conv + taps[row : row + 1] * projected[HALO - WINDOW - j : HALO + ROWS - j]
        qkv[part] = dot(conv.astype(BF), unpack).astype(BF)
    q_at = lax.broadcasted_iota(jnp.int32, (64, 128), 0)
    k_at = lax.broadcasted_iota(jnp.int32, (64, 128), 1) - WINDOW
    band = (k_at <= q_at) & (k_at > q_at - WINDOW)
    for h in range(QHEADS):
        lanes = slice(128 * h, 128 * (h + 1))
        for tile in range(4):
            at = 64 * tile
            q = qkv[0, WINDOW + at : WINDOW + at + 64, lanes]
            k = qkv[1, at : at + 128, lanes]
            v = qkv[2, at : at + 128, lanes]
            logits = dot(q, k, ((1,), (1,))) * HEAD ** (-0.5)
            allowed = (band & ((k_at >= 0) | jnp.logical_not(first_block))) if tile == 0 else band
            logits = jnp.where(allowed, logits, -jnp.inf)
            top = jnp.max(logits, axis=1, keepdims=True)
            weights = jnp.exp(logits - top)
            attention = (weights / jnp.sum(weights, axis=1, keepdims=True)).astype(BF)
            wide[at : at + 64, lanes] = dot(attention, v).astype(BF)


def layer_two_kernel(
    live, residual, halo, gain, taps, taps_others, win, win_others, wout, wout_others, out,
    weights, weights_out, xn, qkv, wide, total, sems,
):
    def pair(own, others, buf, k0):
        return [pltpu.make_async_copy(own, buf.at[0], sems.at[k0])] + [
            pltpu.make_async_copy(others.at[k], buf.at[k + 1], sems.at[k0 + k + 1])
            for k in range(3)
        ]

    first_copies = pair(win, win_others, weights, 0)
    second_copies = pair(wout, wout_others, weights_out, 4)
    for a, b in zip(first_copies, second_copies):
        a.start()
        b.start()
    seq = lax.axis_index("seq")
    first_block = seq == 0
    before = halo[...]
    xn[:HALO] = normed(jnp.where(first_block, jnp.zeros_like(before), before), gain[...])
    xn[HALO:] = normed(residual[...], gain[...])
    pack, unpack = pack_heads(), unpack_heads()
    for d in range(QUARTERS):
        tap = taps[...] if d == 0 else taps_others[d - 1]
        first_copies[d].wait()
        layer_two_quarter(first_block, xn[...], weights.at[d], tap, unpack, qkv, wide)
        mixed = dot(wide[...], pack).astype(BF)
        second_copies[d].wait()
        part = dot(mixed, weights_out[d]).astype(BF).astype(F32)
        total[...] = part if d == 0 else total[...] + part
    row = lax.broadcasted_iota(jnp.int32, (ROWS, 1), 0) + seq * ROWS
    result = (residual[...].astype(F32) + total[...]).astype(BF)
    result = jnp.where(row < live[0], result, jnp.zeros_like(result))
    out[...] = dot(row_order(False), result).astype(BF).reshape(QUARTERS, 64, D)


def layer_two(live, residual, halo, gain, taps, taps_others, win, win_others, wout, wout_others):
    return pl.pallas_call(
        layer_two_kernel,
        out_shape=jax.ShapeDtypeStruct((QUARTERS, 64, D), BF),
        in_specs=[pl.BlockSpec(memory_space=pltpu.SMEM)] + [VM] * 5 + [ANY] * 4,
        out_specs=VM,
        scratch_shapes=[
            pltpu.VMEM((QUARTERS, D, 1344), BF),
            pltpu.VMEM((QUARTERS, 448, D), BF),
            pltpu.VMEM((ROWS + HALO, D), BF),
            pltpu.VMEM((3, ROWS + WINDOW, 512), BF),
            pltpu.VMEM((ROWS, 512), BF),
            pltpu.VMEM((ROWS, D), F32),
            pltpu.SemaphoreType.DMA((8,)),
        ],
        compiler_params=pltpu.CompilerParams(vmem_limit_bytes=60 << 20),
        name="layer_two",
    )(live, residual, halo, gain, taps, taps_others, win, win_others, wout, wout_others)


def on_device(
    pool, page_table, reassign, lengths, gain_one, w_featmap, w_value, w_out_one,
    gain_two, w_window, conv_window, w_out_two,
):
    groups = 32
    device_place = lax.axis_index(("dp", "seq"))
    seq, core, z = lax.axis_index("seq"), lax.axis_index("dp"), lax.axis_index("tensor")
    pages_dev, page_share = pool.shape[:2]
    table = page_table[reassign]
    source = table.reshape(2, 4, 16, 16).transpose(0, 2, 1, 3).reshape(groups, pages_dev)
    owner, slot_of = source // pages_dev, source % pages_dev
    before = jnp.arange(pages_dev)[None, :] < jnp.arange(pages_dev)[:, None]
    rank = jnp.sum((owner[:, :, None] == owner[:, None, :]) & before[None], axis=2)
    hit = (owner == device_place)[:, None, :] & (rank[:, None, :] == jnp.arange(2)[None, :, None])
    send_slot = jnp.sum(jnp.where(hit, slot_of[:, None, :], 0), axis=2)
    outgoing = jnp.take(pool, send_slot.reshape(-1), axis=0).reshape(groups, 2, page_share, D)
    arrived = lax.all_to_all(outgoing, ("dp", "seq"), split_axis=0, concat_axis=0, tiled=True)
    pick = owner[device_place] * 2 + rank[device_place]
    tokens = jnp.take(arrived.reshape(groups * 2, page_share, D), pick, axis=0)
    arrived = lax.all_to_all(
        tokens.reshape(QUARTERS, 64, D), "tensor", split_axis=0, concat_axis=0, tiled=True
    )
    values = jnp.pad(w_value.reshape(D, QHEADS, HEAD), ((0, 0), (0, 0), (0, 16)))
    one = jnp.concatenate([w_featmap.reshape(D, 128), values.reshape(D, 512)], axis=1)
    win = w_window.reshape(D, 1344)
    taps = jnp.pad(conv_window.reshape(9, 448), ((0, 7), (0, 0)))
    kinds = (("r", (D, 640)), ("c", (448, D)), ("r", (D, 1344)), ("c", (448, D)))
    one_g, out_one_g, win_g, out_two_g, taps_g = gather_weights(
        kinds, [one, w_out_one, win, w_out_two], taps
    )
    x, nd, phi, state = layer_one_local(arrived, gain_one[None], one, one_g)
    blocks = lax.all_to_all(state, "seq", split_axis=0, concat_axis=0, tiled=True).astype(F32)
    prefix = [jnp.zeros_like(blocks[0])]
    for k in range(15):
        prefix.append(prefix[-1] + blocks[k])
    prior = lax.all_to_all(
        jnp.stack(prefix).astype(BF), "seq", split_axis=0, concat_axis=0, tiled=True
    )
    residual = layer_one_mix(x, nd, phi, prior, w_out_one, out_one_g)
    halo = lax.ppermute(residual[ROWS - HALO :], "seq", [(i, i + 1) for i in range(15)])
    live = lengths[reassign[core * 4 + z]][None]
    result = layer_two(
        live, residual, halo, gain_two[None], taps, taps_g, win, win_g, w_out_two, out_two_g
    )
    result = lax.all_to_all(result, "tensor", split_axis=0, concat_axis=0, tiled=True)
    return result.reshape(4, 16, 4, D)


def solution(mesh):
    return jax.shard_map(
        on_device,
        mesh=mesh,
        in_specs=(
            P(("dp", "seq"), "tensor", None),
            P(),
            P(),
            P(),
            P(),
            P(None, None, "tensor"),
            P(None, "tensor"),
            P("tensor", None),
            P(),
            P(None, None, "tensor"),
            P(None, None, "tensor"),
            P("tensor", None),
        ),
        out_specs=P("dp", "seq", "tensor", None),
        check_vma=False,
    )
```

```python
import functools

import jax
import jax.numpy as jnp
from jax import lax
from jax.experimental import pallas as pl
from jax.experimental.pallas import tpu as pltpu
from jax.sharding import PartitionSpec as P

HEAD = 112
FEAT = 16
WINDOW = 64
D = 1792
ROWS = 256
HALO = 80
QUARTERS = 4
QHEADS = 4
STATE = 176
NORM_EPS = 1e-05
MESH = pl.DeviceIdType.MESH
BF = jnp.bfloat16
F32 = jnp.float32
ANY = pl.BlockSpec(memory_space=pl.ANY)
VM = pl.BlockSpec(memory_space=pltpu.VMEM)


def dot(a, b, dims=((1,), (0,))):
    return lax.dot_general(a, b, (dims, ((), ())), preferred_element_type=F32)


def places():
    core, seq, z = lax.axis_index("dp"), lax.axis_index("seq"), lax.axis_index("tensor")
    return core, seq, z, seq // 4, seq % 4


class Sender:
    def __init__(self, send_sems, recv_sems):
        self.send_sems, self.recv_sems, self.copies = send_sems, recv_sems, []

    def __call__(self, src, dst, peer):
        k = len(self.copies)
        copy = pltpu.make_async_remote_copy(
            src_ref=src,
            dst_ref=dst,
            send_sem=self.send_sems.at[k],
            recv_sem=self.recv_sems.at[k],
            device_id=peer,
            device_id_type=MESH,
        )
        copy.start()
        self.copies.append(copy)
        return copy


class Chunk:
    def __init__(self, own, others, base, start, count, cols, by_cols):
        self.own, self.others, self.base = own, others, base
        self.start, self.count, self.cols, self.by_cols = start, count, cols, by_cols

    def window(self, core, q, half):
        if self.by_cols:
            n = self.count // 4
            rows = pl.ds(pl.multiple_of(self.start + q * n, 16), n)
            at, width = core * (self.cols // 2), self.cols // 2
            if half is not None:
                cut = (width // 128 + 1) // 2 * 128
                at, width = (at, cut) if half == 0 else (at + cut, width - cut)
            return rows, pl.ds(pl.multiple_of(at, 128), width)
        n = self.count // 8
        at = self.start + core * (self.count // 2) + q * n
        if half is not None:
            n //= 2
            at = at + half * n
        return pl.ds(pl.multiple_of(at, 16), n), slice(None)

    def mine(self, core, q):
        return self.own.at[self.window(core, q, None)]

    def one(self, d, core, q, half=None):
        return self.others.at[(self.base + d - 1,) + self.window(core, q, half)]

    def all(self, core, q, half=None):
        return self.others.at[(pl.ds(self.base, 3),) + self.window(core, q, half)]


class Gather:
    def __init__(self, chunks, send):
        core, seq, z, y, x = places()
        p = jnp.where(core == 0, x, y)

        def at(k):
            q = (p + k) % 4
            return (core, jnp.where(core == 0, y * 4 + q, q * 4 + x), z)

        self.core, self.p, self.send, self.chunks = core, p, send, chunks
        self.up, self.down = (core, seq, (z + 1) % 4), (core, seq, (z + 3) % 4)
        self.right, self.left, self.other = at(1), at(3), (1 - core, seq, z)
        self.now = 0
        self.state = [{} for _ in chunks]

    def q(self, k):
        return (self.p + k) % 4

    def along(self, i, k, half, peer):
        part = self.chunks[i].all(self.core, self.q(k), half)
        return self.send(part, part, peer)

    def stage0(self, i):
        c = self.chunks[i]
        mine = c.mine(self.core, self.p)
        self.state[i]["z"] = (
            self.send(mine, c.one(1, self.core, self.p), self.down),
            self.send(mine, c.one(3, self.core, self.p), self.up),
        )

    def stage1(self, i):
        c, st = self.chunks[i], self.state[i]
        core, p = self.core, self.p
        st["z"][0].wait_recv()
        low = self.send(c.one(1, core, p, 0), c.one(2, core, p, 0), self.down)
        st["z"][1].wait_recv()
        high = self.send(c.one(3, core, p, 1), c.one(2, core, p, 1), self.up)
        st["far"] = (low, high)

    def stage2(self, i):
        st = self.state[i]
        for copy in st["far"]:
            copy.wait_recv()
        st["ring"] = (self.along(i, 0, None, self.right), self.along(i, 0, None, self.left))
        st["last"] = [self.along(i, 0, None, self.other)]

    def stage3(self, i):
        st = self.state[i]
        st["ring"][0].wait_recv()
        low = self.along(i, 3, 0, self.right)
        st["last"].append(self.along(i, 3, None, self.other))
        st["ring"][1].wait_recv()
        high = self.along(i, 1, 1, self.left)
        st["last"].append(self.along(i, 1, None, self.other))
        st["ends"] = (low, high)

    def stage4(self, i):
        st = self.state[i]
        for copy in st["ends"]:
            copy.wait_recv()
        st["last"].append(self.along(i, 2, None, self.other))

    def tick(self, times=1):
        for _ in range(times):
            t = self.now
            if t >= len(self.chunks) + 4:
                return
            for lag in (2, 3, 4, 1, 0):
                if 0 <= t - lag < len(self.chunks):
                    (self.stage0, self.stage1, self.stage2, self.stage3, self.stage4)[lag](t - lag)
            self.now += 1

    def need(self, i):
        while self.now <= i + 4:
            self.tick()
        for copy in self.state[i].pop("last", ()):
            copy.wait_recv()

    def end(self):
        for i in range(len(self.chunks)):
            self.need(i)


def position_of(sigma):
    return sigma % 64 // 4 * 16 + sigma // 64 * 4 + sigma % 4


def row_order(to_positions):
    a = lax.broadcasted_iota(jnp.int32, (ROWS, ROWS), 0)
    b = lax.broadcasted_iota(jnp.int32, (ROWS, ROWS), 1)
    hit = (position_of(b) == a) if to_positions else (position_of(a) == b)
    return hit.astype(F32).astype(BF)


def normed(values, gain):
    wide = values.astype(F32)
    scale = lax.rsqrt(jnp.mean(wide * wide, axis=-1, keepdims=True) + NORM_EPS)
    return (wide * scale * gain).astype(BF)


def build_spread(spread):
    r = lax.broadcasted_iota(jnp.int32, (128, 256), 0)
    f = lax.broadcasted_iota(jnp.int32, (128, 256), 1)
    i, j = f % 16, (f + f // 16) % 16
    for h in range(QHEADS):
        for side in range(2):
            base = side * 64 + h * 16
            one = (r == base + i) & (f < 160)
            two = (r == base + j) & (f < 144)
            spread[h, side, 0] = one.astype(F32).astype(BF)
            spread[h, side, 1] = two.astype(F32).astype(BF)


def spread_pair(rows, spread, h, side):
    f = lax.broadcasted_iota(jnp.int32, (1, 256), 1)
    one = dot(rows, spread[h, side, 0]) + (f == 160).astype(F32)
    two = dot(rows, spread[h, side, 1]) + ((f >= 144) & (f <= 160)).astype(F32)
    return one * two


def key_weights():
    f = lax.broadcasted_iota(jnp.int32, (1, 256), 1)
    pair = jnp.where((f < 16) | (f >= 128), 1.0 / 32, 1.0 / 16)
    return jnp.where(f < 144, pair, jnp.where(f < 160, 0.25, 1.0)).astype(F32)


def local_layer_one(d, x_normed, weight, spread, nd, phi, state):
    projected = dot(x_normed, weight).astype(BF)
    both = projected[:, :128]
    queries, keys = projected[:, :64], projected[:, 64:128]
    lane = lax.broadcasted_iota(jnp.int32, (ROWS, 64), 1)
    a = lax.broadcasted_iota(jnp.int32, (ROWS, ROWS), 0)
    b = lax.broadcasted_iota(jnp.int32, (ROWS, ROWS), 1)
    ones = (lax.broadcasted_iota(jnp.int32, (ROWS, 128), 1) == HEAD).astype(F32).astype(BF)
    for h in range(QHEADS):
        head = d * QHEADS + h
        mine = jnp.where(lane // 16 == h, queries, jnp.zeros_like(queries))
        s = dot(mine, keys, ((1,), (1,))) * 0.25
        kernel = jnp.where(b <= a, 1.0 + s + 0.5 * s * s, 0.0).astype(BF)
        values = projected[:, 128 * (h + 1) : 128 * (h + 2)] + ones
        nd[head] = dot(kernel, values)
        phi[head] = spread_pair(both, spread, h, 0).astype(BF)
        key_phi = (spread_pair(both, spread, h, 1) * key_weights()).astype(BF)
        state[head] = dot(key_phi, values, ((0,), (0,)))[:STATE].astype(BF)


def pack_heads():
    a = lax.broadcasted_iota(jnp.int32, (512, 448), 0)
    b = lax.broadcasted_iota(jnp.int32, (512, 448), 1)
    hit = (a // 128 == b // HEAD) & (a % 128 == b % HEAD)
    return hit.astype(F32).astype(BF)


def unpack_heads():
    a = lax.broadcasted_iota(jnp.int32, (448, 512), 0)
    b = lax.broadcasted_iota(jnp.int32, (448, 512), 1)
    hit = (b // 128 == a // HEAD) & (b % 128 == a % HEAD)
    return hit.astype(F32).astype(BF)


def layer_one_kernel(
    tokens, gain, one, out_one, win, out_two, taps,
    residual, halo, win_g, out_two_g, taps_g,
    w_one, w_out, arrived, spread, xn, nd, phi, state, blocks, prefix, prior, wide, total,
    send_sems, recv_sems, local_sems, token_sems, state_sems, prior_sems, halo_sems,
):
    core, seq, z, _, _ = places()
    send = Sender(send_sems, recv_sems)
    chunks = [
        Chunk(one, w_one, 1, 0, 768, 640, False),
        Chunk(one, w_one, 1, 768, 1024, 640, False),
        Chunk(out_one, w_out, 1, 0, 448, D, True),
        Chunk(win, win_g, 0, 0, 512, 1344, False),
        Chunk(win, win_g, 0, 512, 512, 1344, False),
        Chunk(win, win_g, 0, 1024, 768, 1344, False),
        Chunk(out_two, out_two_g, 0, 0, 448, D, True),
    ]
    gather = Gather(chunks, send)
    own = [
        pltpu.make_async_copy(one, w_one.at[0], local_sems.at[0]),
        pltpu.make_async_copy(out_one, w_out.at[0], local_sems.at[1]),
        pltpu.make_async_copy(tokens.at[z], arrived.at[z], local_sems.at[2]),
    ]
    for copy in own:
        copy.start()
    barrier = pltpu.get_barrier_semaphore()
    greeted = [(core, seq, (z + k) % 4) for k in (1, 2, 3)] + [(1 - core, seq, z)]
    greeted += [(core, (seq + k) % 16, z) for k in range(1, 16)]
    for peer in greeted:
        pl.semaphore_signal(barrier, inc=1, device_id=peer, device_id_type=MESH)
    pl.semaphore_wait(barrier, len(greeted))

    def copy_to(src, dst, sems, k, peer):
        return pltpu.make_async_remote_copy(
            src_ref=src, dst_ref=dst, send_sem=sems.at[0, k], recv_sem=sems.at[1, k],
            device_id=peer, device_id_type=MESH,
        )

    pages = [
        copy_to(tokens.at[(z + k) % 4], arrived.at[z], token_sems, k, (core, seq, (z + k) % 4))
        for k in (1, 2, 3)
    ]
    for copy in pages:
        copy.start()
    gather.tick()
    small = [
        send(taps, taps_g.at[d - 1], (core, seq, (z + 4 - d) % 4)) for d in (1, 2, 3)
    ]
    build_spread(spread)
    gather.tick()
    own[2].wait()
    for copy in pages:
        copy.wait_recv()
    residual[...] = dot(row_order(True), arrived[...].reshape(ROWS, D)).astype(BF)
    xn[...] = normed(residual[...], gain[...])
    gather.tick()
    for d in range(QUARTERS):
        if d == 0:
            own[0].wait()
        else:
            gather.need(0)
            gather.need(1)
        local_layer_one(d, xn[...], w_one[d], spread, nd, phi, state)
        gather.tick()
    mine = pltpu.make_async_copy(state.at[seq], blocks.at[seq], local_sems.at[2])
    mine.start()
    going = []
    for k in range(1, 16):
        peer = (seq + k) % 16
        going.append(copy_to(state.at[peer], blocks.at[seq], state_sems, k, (core, peer, z)))
    for copy in going:
        copy.start()
    gather.tick()
    mine.wait()
    for copy in going:
        copy.wait_recv()
    prefix[0] = jnp.zeros((STATE, 128), BF)

    def add(b, before):
        now = before + blocks[b].astype(F32)
        prefix[b + 1] = now.astype(BF)
        return now

    lax.fori_loop(0, 15, add, jnp.zeros((STATE, 128), F32))
    mine = pltpu.make_async_copy(prefix.at[seq], prior.at[seq], local_sems.at[2])
    mine.start()
    coming = []
    for k in range(1, 16):
        peer = (seq + k) % 16
        coming.append(copy_to(prefix.at[peer], prior.at[seq], prior_sems, k, (core, peer, z)))
    for copy in coming:
        copy.start()
    gather.tick()
    pack = pack_heads()
    mine.wait()
    for copy in coming:
        copy.wait_recv()
    for d in range(QUARTERS):
        for h in range(QHEADS):
            head = d * QHEADS + h
            both = nd[head] + dot(phi[head][:, :STATE], prior[head])
            mixed = both / both[:, HEAD : HEAD + 1]
            wide[:, 128 * h : 128 * (h + 1)] = mixed.astype(BF)
        mixed = dot(wide[...], pack).astype(BF)
        if d == 0:
            own[1].wait()
        else:
            gather.need(2)
        part = dot(mixed, w_out[d]).astype(BF).astype(F32)
        total[...] = part if d == 0 else total[...] + part
        gather.tick()
    residual[...] = (residual[...].astype(F32) + total[...]).astype(BF)
    hand_on = copy_to(
        residual.at[pl.ds(ROWS - HALO, HALO)], halo, halo_sems, 0, (core, (seq + 1) % 16, z)
    )
    hand_on.start()
    gather.end()
    hand_on.wait()
    for copy in small:
        copy.wait_recv()
    for copy in pages + going + coming + send.copies:
        copy.wait_send()


def layer_one(tokens, gain, one, out_one, win, out_two, taps):
    heads = QUARTERS * QHEADS
    bulk = 7 * 12 + 3
    dma = pltpu.SemaphoreType.DMA
    return pl.pallas_call(
        layer_one_kernel,
        out_shape=[
            jax.ShapeDtypeStruct((ROWS, D), BF),
            jax.ShapeDtypeStruct((HALO, D), BF),
            jax.ShapeDtypeStruct((3, D, 1344), BF),
            jax.ShapeDtypeStruct((3, 448, D), BF),
            jax.ShapeDtypeStruct((3, 16, 448), F32),
        ],
        in_specs=[VM, VM] + [ANY] * 5,
        out_specs=[VM, VM] + [ANY] * 3,
        scratch_shapes=[
            pltpu.VMEM((QUARTERS, D, 640), BF),
            pltpu.VMEM((QUARTERS, 448, D), BF),
            pltpu.VMEM((QUARTERS, 64, D), BF),
            pltpu.VMEM((QHEADS, 2, 2, 128, 256), BF),
            pltpu.VMEM((ROWS, D), BF),
            pltpu.VMEM((heads, ROWS, 128), F32),
            pltpu.VMEM((heads, ROWS, 256), BF),
            pltpu.VMEM((heads, STATE, 128), BF),
            pltpu.VMEM((16, STATE, 128), BF),
            pltpu.VMEM((16, STATE, 128), BF),
            pltpu.VMEM((heads, STATE, 128), BF),
            pltpu.VMEM((ROWS, 512), BF),
            pltpu.VMEM((ROWS, D), F32),
            dma((bulk,)),
            dma((bulk,)),
            dma((3,)),
            dma((2, 4)),
            dma((2, 16)),
            dma((2, 16)),
            dma((2, 1)),
        ],
        compiler_params=pltpu.CompilerParams(
            collective_id=0, has_side_effects=True, vmem_limit_bytes=52 << 20
        ),
        name="layer_one",
    )(tokens, gain, one, out_one, win, out_two, taps)


def layer_two_quarter(first_block, xn, weight, taps, unpack, qkv, wide):
    span = ROWS + WINDOW
    for part in range(3):
        cols = slice(448 * part, 448 * (part + 1))
        projected = dot(xn, weight[:, cols])
        conv = taps[part : part + 1] * projected[HALO - WINDOW :]
        for j in (1, 2):
            row = 3 * j + part
            conv = conv + taps[row : row + 1] * projected[HALO - WINDOW - j : HALO + ROWS - j]
        qkv[part] = dot(conv.astype(BF), unpack).astype(BF)
    q_at = lax.broadcasted_iota(jnp.int32, (64, 128), 0)
    k_at = lax.broadcasted_iota(jnp.int32, (64, 128), 1) - WINDOW
    band = (k_at <= q_at) & (k_at > q_at - WINDOW)
    for h in range(QHEADS):
        lanes = slice(128 * h, 128 * (h + 1))
        for tile in range(4):
            at = 64 * tile
            q = qkv[0, WINDOW + at : WINDOW + at + 64, lanes]
            k = qkv[1, at : at + 128, lanes]
            v = qkv[2, at : at + 128, lanes]
            logits = dot(q, k, ((1,), (1,))) * HEAD ** (-0.5)
            allowed = (band & ((k_at >= 0) | jnp.logical_not(first_block))) if tile == 0 else band
            logits = jnp.where(allowed, logits, -jnp.inf)
            top = jnp.max(logits, axis=1, keepdims=True)
            weights = jnp.exp(logits - top)
            attention = (weights / jnp.sum(weights, axis=1, keepdims=True)).astype(BF)
            wide[at : at + 64, lanes] = dot(attention, v).astype(BF)


def layer_two_kernel(
    live, residual, halo, gain, taps, taps_others, win, win_others, wout, wout_others, out,
    weights, weights_out, xn, qkv, wide, total, sems,
):
    def pair(own, others, buf, k0):
        return [pltpu.make_async_copy(own, buf.at[0], sems.at[k0])] + [
            pltpu.make_async_copy(others.at[k], buf.at[k + 1], sems.at[k0 + k + 1])
            for k in range(3)
        ]

    first_copies = pair(win, win_others, weights, 0)
    second_copies = pair(wout, wout_others, weights_out, 4)
    for a, b in zip(first_copies, second_copies):
        a.start()
        b.start()
    seq = lax.axis_index("seq")
    first_block = seq == 0
    before = halo[...]
    xn[:HALO] = normed(jnp.where(first_block, jnp.zeros_like(before), before), gain[...])
    xn[HALO:] = normed(residual[...], gain[...])
    pack, unpack = pack_heads(), unpack_heads()
    for d in range(QUARTERS):
        tap = taps[...] if d == 0 else taps_others[d - 1]
        first_copies[d].wait()
        layer_two_quarter(first_block, xn[...], weights.at[d], tap, unpack, qkv, wide)
        mixed = dot(wide[...], pack).astype(BF)
        second_copies[d].wait()
        part = dot(mixed, weights_out[d]).astype(BF).astype(F32)
        total[...] = part if d == 0 else total[...] + part
    row = lax.broadcasted_iota(jnp.int32, (ROWS, 1), 0) + seq * ROWS
    result = (residual[...].astype(F32) + total[...]).astype(BF)
    result = jnp.where(row < live[0], result, jnp.zeros_like(result))
    out[...] = dot(row_order(False), result).astype(BF).reshape(QUARTERS, 64, D)


def layer_two(live, residual, halo, gain, taps, taps_others, win, win_others, wout, wout_others):
    return pl.pallas_call(
        layer_two_kernel,
        out_shape=jax.ShapeDtypeStruct((QUARTERS, 64, D), BF),
        in_specs=[pl.BlockSpec(memory_space=pltpu.SMEM)] + [VM] * 5 + [ANY] * 4,
        out_specs=VM,
        scratch_shapes=[
            pltpu.VMEM((QUARTERS, D, 1344), BF),
            pltpu.VMEM((QUARTERS, 448, D), BF),
            pltpu.VMEM((ROWS + HALO, D), BF),
            pltpu.VMEM((3, ROWS + WINDOW, 512), BF),
            pltpu.VMEM((ROWS, 512), BF),
            pltpu.VMEM((ROWS, D), F32),
            pltpu.SemaphoreType.DMA((8,)),
        ],
        compiler_params=pltpu.CompilerParams(vmem_limit_bytes=60 << 20),
        name="layer_two",
    )(live, residual, halo, gain, taps, taps_others, win, win_others, wout, wout_others)


def on_device(
    pool, page_table, reassign, lengths, gain_one, w_featmap, w_value, w_out_one,
    gain_two, w_window, conv_window, w_out_two,
):
    groups = 32
    device_place = lax.axis_index(("dp", "seq"))
    seq, core, z = lax.axis_index("seq"), lax.axis_index("dp"), lax.axis_index("tensor")
    pages_dev, page_share = pool.shape[:2]
    table = page_table[reassign]
    source = table.reshape(2, 4, 16, 16).transpose(0, 2, 1, 3).reshape(groups, pages_dev)
    owner, slot_of = source // pages_dev, source % pages_dev
    before = jnp.arange(pages_dev)[None, :] < jnp.arange(pages_dev)[:, None]
    rank = jnp.sum((owner[:, :, None] == owner[:, None, :]) & before[None], axis=2)
    hit = (owner == device_place)[:, None, :] & (rank[:, None, :] == jnp.arange(2)[None, :, None])
    send_slot = jnp.sum(jnp.where(hit, slot_of[:, None, :], 0), axis=2)
    outgoing = jnp.take(pool, send_slot.reshape(-1), axis=0).reshape(groups, 2, page_share, D)
    arrived = lax.all_to_all(outgoing, ("dp", "seq"), split_axis=0, concat_axis=0, tiled=True)
    pick = owner[device_place] * 2 + rank[device_place]
    tokens = jnp.take(arrived.reshape(groups * 2, page_share, D), pick, axis=0)
    tokens = tokens.reshape(QUARTERS, 64, D)
    values = jnp.pad(w_value.reshape(D, QHEADS, HEAD), ((0, 0), (0, 0), (0, 16)))
    one = jnp.concatenate([w_featmap.reshape(D, 128), values.reshape(D, 512)], axis=1)
    win = w_window.reshape(D, 1344)
    taps = jnp.pad(conv_window.reshape(9, 448), ((0, 7), (0, 0)))
    residual, halo, win_g, out_two_g, taps_g = layer_one(
        tokens, gain_one[None], one, w_out_one, win, w_out_two, taps
    )
    live = lengths[reassign[core * 4 + z]][None]
    result = layer_two(
        live, residual, halo, gain_two[None], taps, taps_g, win, win_g, w_out_two, out_two_g
    )
    result = lax.all_to_all(result, "tensor", split_axis=0, concat_axis=0, tiled=True)
    return result.reshape(4, 16, 4, D)


def solution(mesh):
    return jax.shard_map(
        on_device,
        mesh=mesh,
        in_specs=(
            P(("dp", "seq"), "tensor", None),
            P(),
            P(),
            P(),
            P(),
            P(None, None, "tensor"),
            P(None, "tensor"),
            P("tensor", None),
            P(),
            P(None, None, "tensor"),
            P(None, None, "tensor"),
            P("tensor", None),
        ),
        out_specs=P("dp", "seq", "tensor", None),
        check_vma=False,
    )
```

```python
import functools

import jax
import jax.numpy as jnp
from jax import lax
from jax.experimental import pallas as pl
from jax.experimental.pallas import tpu as pltpu
from jax.sharding import PartitionSpec as P

HEAD = 112
FEAT = 16
WINDOW = 64
D = 1792
ROWS = 256
HALO = 80
QUARTERS = 4
QHEADS = 4
STATE = 176
NORM_EPS = 1e-05
MESH = pl.DeviceIdType.MESH
BF = jnp.bfloat16
F32 = jnp.float32
ANY = pl.BlockSpec(memory_space=pl.ANY)
VM = pl.BlockSpec(memory_space=pltpu.VMEM)


def dot(a, b, dims=((1,), (0,))):
    return lax.dot_general(a, b, (dims, ((), ())), preferred_element_type=F32)


def places():
    core, seq, z = lax.axis_index("dp"), lax.axis_index("seq"), lax.axis_index("tensor")
    return core, seq, z, seq // 4, seq % 4


class Sender:
    def __init__(self, send_sems, recv_sems):
        self.send_sems, self.recv_sems, self.copies = send_sems, recv_sems, []

    def __call__(self, src, dst, peer):
        k = len(self.copies)
        copy = pltpu.make_async_remote_copy(
            src_ref=src,
            dst_ref=dst,
            send_sem=self.send_sems.at[k],
            recv_sem=self.recv_sems.at[k],
            device_id=peer,
            device_id_type=MESH,
        )
        copy.start()
        self.copies.append(copy)
        return copy


class Chunk:
    def __init__(self, own, others, base, start, count, cols, by_cols):
        self.own, self.others, self.base = own, others, base
        self.start, self.count, self.cols, self.by_cols = start, count, cols, by_cols

    def window(self, core, q, half):
        if self.by_cols:
            n = self.count // 4
            rows = pl.ds(pl.multiple_of(self.start + q * n, 16), n)
            at, width = core * (self.cols // 2), self.cols // 2
            if half is not None:
                cut = (width // 128 + 1) // 2 * 128
                at, width = (at, cut) if half == 0 else (at + cut, width - cut)
            return rows, pl.ds(pl.multiple_of(at, 128), width)
        n = self.count // 8
        at = self.start + core * (self.count // 2) + q * n
        if half is not None:
            n //= 2
            at = at + half * n
        return pl.ds(pl.multiple_of(at, 16), n), slice(None)

    def mine(self, core, q):
        return self.own.at[self.window(core, q, None)]

    def one(self, d, core, q, half=None):
        return self.others.at[(self.base + d - 1,) + self.window(core, q, half)]

    def all(self, core, q, half=None):
        return self.others.at[(pl.ds(self.base, 3),) + self.window(core, q, half)]


class Gather:
    def __init__(self, chunks, send):
        core, seq, z, y, x = places()
        p = jnp.where(core == 0, x, y)

        def at(k):
            q = (p + k) % 4
            return (core, jnp.where(core == 0, y * 4 + q, q * 4 + x), z)

        self.core, self.p, self.send, self.chunks = core, p, send, chunks
        self.up, self.down = (core, seq, (z + 1) % 4), (core, seq, (z + 3) % 4)
        self.right, self.left, self.other = at(1), at(3), (1 - core, seq, z)
        self.now = 0
        self.state = [{} for _ in chunks]

    def q(self, k):
        return (self.p + k) % 4

    def along(self, i, k, half, peer):
        part = self.chunks[i].all(self.core, self.q(k), half)
        return self.send(part, part, peer)

    def stage0(self, i):
        c = self.chunks[i]
        mine = c.mine(self.core, self.p)
        self.state[i]["z"] = (
            self.send(mine, c.one(1, self.core, self.p), self.down),
            self.send(mine, c.one(3, self.core, self.p), self.up),
        )

    def stage1(self, i):
        c, st = self.chunks[i], self.state[i]
        core, p = self.core, self.p
        st["z"][0].wait_recv()
        low = self.send(c.one(1, core, p, 0), c.one(2, core, p, 0), self.down)
        st["z"][1].wait_recv()
        high = self.send(c.one(3, core, p, 1), c.one(2, core, p, 1), self.up)
        st["far"] = (low, high)

    def stage2(self, i):
        st = self.state[i]
        for copy in st["far"]:
            copy.wait_recv()
        st["ring"] = (self.along(i, 0, None, self.right), self.along(i, 0, None, self.left))
        st["last"] = [self.along(i, 0, None, self.other)]

    def stage3(self, i):
        st = self.state[i]
        st["ring"][0].wait_recv()
        low = self.along(i, 3, 0, self.right)
        st["last"].append(self.along(i, 3, None, self.other))
        st["ring"][1].wait_recv()
        high = self.along(i, 1, 1, self.left)
        st["last"].append(self.along(i, 1, None, self.other))
        st["ends"] = (low, high)

    def stage4(self, i):
        st = self.state[i]
        for copy in st["ends"]:
            copy.wait_recv()
        st["last"].append(self.along(i, 2, None, self.other))

    def tick(self, times=1):
        for _ in range(times):
            t = self.now
            if t >= len(self.chunks) + 4:
                return
            for lag in (2, 3, 4, 1, 0):
                if 0 <= t - lag < len(self.chunks):
                    (self.stage0, self.stage1, self.stage2, self.stage3, self.stage4)[lag](t - lag)
            self.now += 1

    def need(self, i):
        while self.now <= i + 4:
            self.tick()
        for copy in self.state[i].pop("last", ()):
            copy.wait_recv()

    def end(self):
        for i in range(len(self.chunks)):
            self.need(i)


def position_of(sigma):
    return sigma % 64 // 4 * 16 + sigma // 64 * 4 + sigma % 4


def row_order(to_positions):
    a = lax.broadcasted_iota(jnp.int32, (ROWS, ROWS), 0)
    b = lax.broadcasted_iota(jnp.int32, (ROWS, ROWS), 1)
    hit = (position_of(b) == a) if to_positions else (position_of(a) == b)
    return hit.astype(F32).astype(BF)


def normed(values, gain):
    wide = values.astype(F32)
    scale = lax.rsqrt(jnp.mean(wide * wide, axis=-1, keepdims=True) + NORM_EPS)
    return (wide * scale * gain).astype(BF)


def build_spread(spread):
    r = lax.broadcasted_iota(jnp.int32, (128, 256), 0)
    f = lax.broadcasted_iota(jnp.int32, (128, 256), 1)
    i, j = f % 16, (f + f // 16) % 16
    for h in range(QHEADS):
        for side in range(2):
            base = side * 64 + h * 16
            one = (r == base + i) & (f < 160)
            two = (r == base + j) & (f < 144)
            spread[side, 0, :, 256 * h : 256 * (h + 1)] = one.astype(F32).astype(BF)
            spread[side, 1, :, 256 * h : 256 * (h + 1)] = two.astype(F32).astype(BF)


def features(rows, spread, side):
    f = lax.broadcasted_iota(jnp.int32, (1, 256 * QHEADS), 1) % 256
    one = dot(rows, spread[side, 0]) + (f == 160).astype(F32)
    two = dot(rows, spread[side, 1]) + ((f >= 144) & (f <= 160)).astype(F32)
    return one * two


def key_weights():
    f = lax.broadcasted_iota(jnp.int32, (1, 256 * QHEADS), 1) % 256
    pair = jnp.where((f < 16) | (f >= 128), 1.0 / 32, 1.0 / 16)
    return jnp.where(f < 144, pair, jnp.where(f < 160, 0.25, 1.0)).astype(F32)


def local_layer_one(d, x_normed, weight, spread, nd, phi, state):
    projected = dot(x_normed, weight).astype(BF)
    both = projected[:, :128]
    queries, keys = projected[:, :64], projected[:, 64:128]
    lane = lax.broadcasted_iota(jnp.int32, (ROWS, 64), 1)
    a = lax.broadcasted_iota(jnp.int32, (ROWS, ROWS), 0)
    b = lax.broadcasted_iota(jnp.int32, (ROWS, ROWS), 1)
    ones = (lax.broadcasted_iota(jnp.int32, (ROWS, 128), 1) == HEAD).astype(F32).astype(BF)
    values = [projected[:, 128 * (h + 1) : 128 * (h + 2)] + ones for h in range(QHEADS)]
    kernels = []
    for h in range(QHEADS):
        mine = jnp.where(lane // 16 == h, queries, jnp.zeros_like(queries))
        s = dot(mine, keys, ((1,), (1,))) * 0.25
        kernels.append(jnp.where(b <= a, 1.0 + s + 0.5 * s * s, 0.0).astype(BF))
    key_phi = (features(both, spread, 1) * key_weights()).astype(BF)
    phi[d] = features(both, spread, 0).astype(BF)
    for h in range(QHEADS):
        cols = slice(256 * h, 256 * (h + 1))
        state[d * QHEADS + h] = dot(key_phi[:, cols], values[h], ((0,), (0,)))[:STATE].astype(BF)
    for h in range(QHEADS):
        nd[d, :, 128 * h : 128 * (h + 1)] = dot(kernels[h], values[h])


def mix_heads(d, nd, phi, prior, wide):
    full = [
        nd[d, :, 128 * h : 128 * (h + 1)]
        + dot(phi[d, :, 256 * h : 256 * h + STATE], prior[d * QHEADS + h])
        for h in range(QHEADS)
    ]
    for h in range(QHEADS):
        wide[:, 128 * h : 128 * (h + 1)] = (full[h] / full[h][:, HEAD : HEAD + 1]).astype(BF)


def pack_heads():
    a = lax.broadcasted_iota(jnp.int32, (512, 448), 0)
    b = lax.broadcasted_iota(jnp.int32, (512, 448), 1)
    hit = (a // 128 == b // HEAD) & (a % 128 == b % HEAD)
    return hit.astype(F32).astype(BF)


def unpack_heads():
    a = lax.broadcasted_iota(jnp.int32, (448, 512), 0)
    b = lax.broadcasted_iota(jnp.int32, (448, 512), 1)
    hit = (b // 128 == a // HEAD) & (b % 128 == a % HEAD)
    return hit.astype(F32).astype(BF)


def layer_one_kernel(
    wanted, gain, outgoing, one, out_one, win, out_two, taps,
    residual, halo, win_g, out_two_g, taps_g,
    w_one, w_out, pages, tokens, arrived, spread, xn, nd, phi, state, blocks, prefix, prior, wide, total,
    send_sems, recv_sems, local_sems, page_sems, token_sems, state_sems, prior_sems, halo_sems,
):
    core, seq, z, _, _ = places()
    send = Sender(send_sems, recv_sems)
    chunks = [
        Chunk(one, w_one, 1, 0, 768, 640, False),
        Chunk(one, w_one, 1, 768, 1024, 640, False),
        Chunk(out_one, w_out, 1, 0, 448, D, True),
        Chunk(win, win_g, 0, 0, 512, 1344, False),
        Chunk(win, win_g, 0, 512, 512, 1344, False),
        Chunk(win, win_g, 0, 1024, 768, 1344, False),
        Chunk(out_two, out_two_g, 0, 0, 448, D, True),
    ]
    gather = Gather(chunks, send)
    own = [
        pltpu.make_async_copy(one, w_one.at[0], local_sems.at[0]),
        pltpu.make_async_copy(out_one, w_out.at[0], local_sems.at[1]),
        pltpu.make_async_copy(outgoing.at[core * 16 + seq], pages.at[core * 16 + seq], local_sems.at[2]),
    ]
    for copy in own:
        copy.start()
    barrier = pltpu.get_barrier_semaphore()
    place = core * 16 + seq
    plane = [((place + k) % 32 // 16, (place + k) % 16, z) for k in range(1, 32)]
    greeted = [(core, seq, (z + k) % 4) for k in (1, 2, 3)] + plane
    for peer in greeted:
        pl.semaphore_signal(barrier, inc=1, device_id=peer, device_id_type=MESH)
    pl.semaphore_wait(barrier, len(greeted))

    def copy_to(src, dst, sems, k, peer):
        return pltpu.make_async_remote_copy(
            src_ref=src, dst_ref=dst, send_sem=sems.at[0, k], recv_sem=sems.at[1, k],
            device_id=peer, device_id_type=MESH,
        )

    page_copies = [
        copy_to(outgoing.at[(place + k) % 32], pages.at[place], page_sems, k, plane[k - 1])
        for k in range(1, 32)
    ]
    for copy in page_copies:
        copy.start()
    gather.tick()
    small = [
        send(taps, taps_g.at[d - 1], (core, seq, (z + 4 - d) % 4)) for d in (1, 2, 3)
    ]
    build_spread(spread)
    gather.tick()
    own[2].wait()
    for copy in page_copies:
        copy.wait_recv()
    column = lax.broadcasted_iota(jnp.int32, (ROWS, ROWS), 1)
    chosen = (wanted[...] == column).astype(F32).astype(BF)
    rows = pages[...].astype(F32).reshape(ROWS, D).astype(BF)
    tokens[...] = dot(chosen, rows).astype(BF).reshape(QUARTERS, 64, D)
    kept = pltpu.make_async_copy(tokens.at[z], arrived.at[z], local_sems.at[2])
    kept.start()
    token_copies = [
        copy_to(tokens.at[(z + k) % 4], arrived.at[z], token_sems, k, (core, seq, (z + k) % 4))
        for k in (1, 2, 3)
    ]
    for copy in token_copies:
        copy.start()
    gather.tick()
    kept.wait()
    for copy in token_copies:
        copy.wait_recv()
    residual[...] = dot(row_order(True), arrived[...].reshape(ROWS, D)).astype(BF)
    xn[...] = normed(residual[...], gain[...])
    gather.tick()
    for d in range(QUARTERS):
        if d == 0:
            own[0].wait()
        else:
            gather.need(0)
            gather.need(1)
        local_layer_one(d, xn[...], w_one[d], spread, nd, phi, state)
        gather.tick()
    mine = pltpu.make_async_copy(state.at[seq], blocks.at[seq], local_sems.at[2])
    mine.start()
    going = []
    for k in range(1, 16):
        peer = (seq + k) % 16
        going.append(copy_to(state.at[peer], blocks.at[seq], state_sems, k, (core, peer, z)))
    for copy in going:
        copy.start()
    gather.tick()
    mine.wait()
    for copy in going:
        copy.wait_recv()
    prefix[0] = jnp.zeros((STATE, 128), BF)

    def add(b, before):
        now = before + blocks[b].astype(F32)
        prefix[b + 1] = now.astype(BF)
        return now

    lax.fori_loop(0, 15, add, jnp.zeros((STATE, 128), F32))
    mine = pltpu.make_async_copy(prefix.at[seq], prior.at[seq], local_sems.at[2])
    mine.start()
    coming = []
    for k in range(1, 16):
        peer = (seq + k) % 16
        coming.append(copy_to(prefix.at[peer], prior.at[seq], prior_sems, k, (core, peer, z)))
    for copy in coming:
        copy.start()
    gather.tick()
    pack = pack_heads()
    mine.wait()
    for copy in coming:
        copy.wait_recv()
    for d in range(QUARTERS):
        mix_heads(d, nd, phi, prior, wide)
        mixed = dot(wide[...], pack).astype(BF)
        if d == 0:
            own[1].wait()
        else:
            gather.need(2)
        part = dot(mixed, w_out[d]).astype(BF).astype(F32)
        total[...] = part if d == 0 else total[...] + part
        gather.tick()
    residual[...] = (residual[...].astype(F32) + total[...]).astype(BF)
    hand_on = copy_to(
        residual.at[pl.ds(ROWS - HALO, HALO)], halo, halo_sems, 0, (core, (seq + 1) % 16, z)
    )
    hand_on.start()
    gather.end()
    hand_on.wait()
    for copy in small:
        copy.wait_recv()
    for copy in page_copies + token_copies + going + coming + send.copies:
        copy.wait_send()


def layer_one(wanted, gain, outgoing, one, out_one, win, out_two, taps):
    heads = QUARTERS * QHEADS
    bulk = 7 * 12 + 3
    dma = pltpu.SemaphoreType.DMA
    return pl.pallas_call(
        layer_one_kernel,
        out_shape=[
            jax.ShapeDtypeStruct((ROWS, D), BF),
            jax.ShapeDtypeStruct((HALO, D), BF),
            jax.ShapeDtypeStruct((3, D, 1344), BF),
            jax.ShapeDtypeStruct((3, 448, D), BF),
            jax.ShapeDtypeStruct((3, 16, 448), F32),
        ],
        in_specs=[VM, VM] + [ANY] * 6,
        out_specs=[VM, VM] + [ANY] * 3,
        scratch_shapes=[
            pltpu.VMEM((QUARTERS, D, 640), BF),
            pltpu.VMEM((QUARTERS, 448, D), BF),
            pltpu.VMEM((32, 8, D), BF),
            pltpu.VMEM((QUARTERS, 64, D), BF),
            pltpu.VMEM((QUARTERS, 64, D), BF),
            pltpu.VMEM((2, 2, 128, 256 * QHEADS), BF),
            pltpu.VMEM((ROWS, D), BF),
            pltpu.VMEM((QUARTERS, ROWS, 512), F32),
            pltpu.VMEM((QUARTERS, ROWS, 1024), BF),
            pltpu.VMEM((heads, STATE, 128), BF),
            pltpu.VMEM((16, STATE, 128), BF),
            pltpu.VMEM((16, STATE, 128), BF),
            pltpu.VMEM((heads, STATE, 128), BF),
            pltpu.VMEM((ROWS, 512), BF),
            pltpu.VMEM((ROWS, D), F32),
            dma((bulk,)),
            dma((bulk,)),
            dma((3,)),
            dma((2, 32)),
            dma((2, 4)),
            dma((2, 16)),
            dma((2, 16)),
            dma((2, 1)),
        ],
        compiler_params=pltpu.CompilerParams(
            collective_id=0, has_side_effects=True, vmem_limit_bytes=52 << 20
        ),
        name="layer_one",
    )(wanted, gain, outgoing, one, out_one, win, out_two, taps)


def layer_two_quarter(first_block, xn, weight, taps, unpack, qkv, wide):
    span = ROWS + WINDOW
    for part in range(3):
        cols = slice(448 * part, 448 * (part + 1))
        projected = dot(xn, weight[:, cols])
        conv = taps[part : part + 1] * projected[HALO - WINDOW :]
        for j in (1, 2):
            row = 3 * j + part
            conv = conv + taps[row : row + 1] * projected[HALO - WINDOW - j : HALO + ROWS - j]
        qkv[part] = dot(conv.astype(BF), unpack).astype(BF)
    q_at = lax.broadcasted_iota(jnp.int32, (64, 128), 0)
    k_at = lax.broadcasted_iota(jnp.int32, (64, 128), 1) - WINDOW
    band = (k_at <= q_at) & (k_at > q_at - WINDOW)
    inside = band & ((k_at >= 0) | jnp.logical_not(first_block))
    tiles = [(h, 64 * t) for h in range(QHEADS) for t in range(4)]
    logits = []
    for h, at in tiles:
        lanes = slice(128 * h, 128 * (h + 1))
        q = qkv[0, WINDOW + at : WINDOW + at + 64, lanes]
        k = qkv[1, at : at + 128, lanes]
        scaled = dot(q, k, ((1,), (1,))) * HEAD ** (-0.5)
        logits.append(jnp.where(band if at else inside, scaled, -jnp.inf))
    logits = jnp.concatenate(logits, axis=0)
    weights = jnp.exp(logits - jnp.max(logits, axis=1, keepdims=True))
    attention = (weights / jnp.sum(weights, axis=1, keepdims=True)).astype(BF)
    for n, (h, at) in enumerate(tiles):
        lanes = slice(128 * h, 128 * (h + 1))
        v = qkv[2, at : at + 128, lanes]
        wide[at : at + 64, lanes] = dot(attention[64 * n : 64 * (n + 1)], v).astype(BF)


def layer_two_kernel(
    live, residual, halo, gain, taps, taps_others, win, win_others, wout, wout_others, out,
    weights, weights_out, xn, qkv, wide, total, result_rows, sems, out_sems,
):
    def pair(own, others, buf, k0):
        return [pltpu.make_async_copy(own, buf.at[0], sems.at[k0])] + [
            pltpu.make_async_copy(others.at[k], buf.at[k + 1], sems.at[k0 + k + 1])
            for k in range(3)
        ]

    first_copies = pair(win, win_others, weights, 0)
    second_copies = pair(wout, wout_others, weights_out, 4)
    for a, b in zip(first_copies, second_copies):
        a.start()
        b.start()
    core, seq, z, _, _ = places()
    peers = [(core, seq, (z + k) % 4) for k in (2, 1, 3)]
    barrier = pltpu.get_barrier_semaphore()
    for peer in peers:
        pl.semaphore_signal(barrier, inc=1, device_id=peer, device_id_type=MESH)
    first_block = seq == 0
    before = halo[...]
    xn[:HALO] = normed(jnp.where(first_block, jnp.zeros_like(before), before), gain[...])
    xn[HALO:] = normed(residual[...], gain[...])
    pack, unpack = pack_heads(), unpack_heads()
    for d in range(QUARTERS):
        tap = taps[...] if d == 0 else taps_others[d - 1]
        first_copies[d].wait()
        layer_two_quarter(first_block, xn[...], weights.at[d], tap, unpack, qkv, wide)
        mixed = dot(wide[...], pack).astype(BF)
        second_copies[d].wait()
        part = dot(mixed, weights_out[d]).astype(BF).astype(F32)
        total[...] = part if d == 0 else total[...] + part
    row = lax.broadcasted_iota(jnp.int32, (ROWS, 1), 0) + seq * ROWS
    result = (residual[...].astype(F32) + total[...]).astype(BF)
    result = jnp.where(row < live[0], result, jnp.zeros_like(result))
    result_rows[...] = dot(row_order(False), result).astype(BF).reshape(QUARTERS, 64, D)
    pl.semaphore_wait(barrier, 3)
    kept = pltpu.make_async_copy(result_rows.at[z], out.at[z], sems.at[0])
    kept.start()
    copies = []
    for n, k in enumerate((2, 1, 3)):
        copy = pltpu.make_async_remote_copy(
            src_ref=result_rows.at[(z + k) % 4], dst_ref=out.at[z], send_sem=out_sems.at[0, n],
            recv_sem=out_sems.at[1, n], device_id=peers[n], device_id_type=MESH,
        )
        copy.start()
        copies.append(copy)
    kept.wait()
    for copy in copies:
        copy.wait()


def layer_two(live, residual, halo, gain, taps, taps_others, win, win_others, wout, wout_others):
    return pl.pallas_call(
        layer_two_kernel,
        out_shape=jax.ShapeDtypeStruct((QUARTERS, 64, D), BF),
        in_specs=[pl.BlockSpec(memory_space=pltpu.SMEM)] + [VM] * 5 + [ANY] * 4,
        out_specs=ANY,
        scratch_shapes=[
            pltpu.VMEM((QUARTERS, D, 1344), BF),
            pltpu.VMEM((QUARTERS, 448, D), BF),
            pltpu.VMEM((ROWS + HALO, D), BF),
            pltpu.VMEM((3, ROWS + WINDOW, 512), BF),
            pltpu.VMEM((ROWS, 512), BF),
            pltpu.VMEM((ROWS, D), F32),
            pltpu.VMEM((QUARTERS, 64, D), BF),
            pltpu.SemaphoreType.DMA((8,)),
            pltpu.SemaphoreType.DMA((2, 3)),
        ],
        compiler_params=pltpu.CompilerParams(
            collective_id=1, has_side_effects=True, vmem_limit_bytes=60 << 20
        ),
        name="layer_two",
    )(live, residual, halo, gain, taps, taps_others, win, win_others, wout, wout_others)


def on_device(
    pool, page_table, reassign, lengths, gain_one, w_featmap, w_value, w_out_one,
    gain_two, w_window, conv_window, w_out_two,
):
    groups = 32
    device_place = lax.axis_index(("dp", "seq"))
    seq, core, z = lax.axis_index("seq"), lax.axis_index("dp"), lax.axis_index("tensor")
    pages_dev, page_share = pool.shape[:2]
    table = page_table[reassign]
    source = table.reshape(2, 4, 16, 16).transpose(0, 2, 1, 3).reshape(groups, pages_dev)
    owner, slot_of = source // pages_dev, source % pages_dev
    before = jnp.arange(pages_dev)[None, :] < jnp.arange(pages_dev)[:, None]
    rank = jnp.sum((owner[:, :, None] == owner[:, None, :]) & before[None], axis=2)
    hit = (owner == device_place)[:, None, :] & (rank[:, None, :] == jnp.arange(2)[None, :, None])
    send_slot = jnp.sum(jnp.where(hit, slot_of[:, None, :], 0), axis=2)
    outgoing = jnp.take(pool, send_slot.reshape(-1), axis=0).reshape(groups, 8, D)
    pick = owner[device_place] * 2 + rank[device_place]
    wanted = (pick[:, None] * 4 + jnp.arange(4)[None, :]).reshape(ROWS, 1)
    values = jnp.pad(w_value.reshape(D, QHEADS, HEAD), ((0, 0), (0, 0), (0, 16)))
    one = jnp.concatenate([w_featmap.reshape(D, 128), values.reshape(D, 512)], axis=1)
    win = w_window.reshape(D, 1344)
    taps = jnp.pad(conv_window.reshape(9, 448), ((0, 7), (0, 0)))
    residual, halo, win_g, out_two_g, taps_g = layer_one(
        wanted, gain_one[None], outgoing, one, w_out_one, win, w_out_two, taps
    )
    live = lengths[reassign[core * 4 + z]][None]
    result = layer_two(
        live, residual, halo, gain_two[None], taps, taps_g, win, win_g, w_out_two, out_two_g
    )
    return result.reshape(4, 16, 4, D)


def solution(mesh):
    return jax.shard_map(
        on_device,
        mesh=mesh,
        in_specs=(
            P(("dp", "seq"), "tensor", None),
            P(),
            P(),
            P(),
            P(),
            P(None, None, "tensor"),
            P(None, "tensor"),
            P("tensor", None),
            P(),
            P(None, None, "tensor"),
            P(None, None, "tensor"),
            P("tensor", None),
        ),
        out_specs=P("dp", "seq", "tensor", None),
        check_vma=False,
    )
```

```python
import functools

import jax
import jax.numpy as jnp
from jax import lax
from jax.experimental import pallas as pl
from jax.experimental.pallas import tpu as pltpu
from jax.sharding import PartitionSpec as P

HEAD = 112
FEAT = 16
WINDOW = 64
D = 1792
ROWS = 256
HALO = 80
QUARTERS = 4
QHEADS = 4
STATE = 176
CHUNKS = ["f", "v0", "v1", "o", "w0", "w1", "w2", "p"]
PLAN = (
    "0f 0v0 0v1 1f 1v0 1v1 2f 2v0 2v1",
    "0o 3f 3v0 3v1",
    "",
    "4f 4v0 4v1 1o 0w0 2o",
    "1w0 0w1",
    "2w0",
    "3o 1w1 0w2",
    "2w1 4o",
    "3w0 1w2 0p",
    "2w2",
    "3w1 4w0",
    "1p",
    "3w2 4w1",
    "4w2 2p",
)
NORM_EPS = 1e-05
MESH = pl.DeviceIdType.MESH
BF = jnp.bfloat16
F32 = jnp.float32
ANY = pl.BlockSpec(memory_space=pl.ANY)
VM = pl.BlockSpec(memory_space=pltpu.VMEM)


def dot(a, b, dims=((1,), (0,))):
    return lax.dot_general(a, b, (dims, ((), ())), preferred_element_type=F32)


def places():
    core, seq, z = lax.axis_index("dp"), lax.axis_index("seq"), lax.axis_index("tensor")
    return core, seq, z, seq // 4, seq % 4


class Sender:
    def __init__(self, send_sems, recv_sems):
        self.send_sems, self.recv_sems, self.copies = send_sems, recv_sems, []

    def __call__(self, src, dst, peer):
        k = len(self.copies)
        copy = pltpu.make_async_remote_copy(
            src_ref=src,
            dst_ref=dst,
            send_sem=self.send_sems.at[k],
            recv_sem=self.recv_sems.at[k],
            device_id=peer,
            device_id_type=MESH,
        )
        copy.start()
        self.copies.append(copy)
        return copy


class Chunk:
    def __init__(self, own, others, base, start, count, cols, by_cols, z_only=False):
        self.own, self.others, self.base = own, others, base
        self.start, self.count, self.cols, self.by_cols = start, count, cols, by_cols
        self.z_only = z_only

    def window(self, core, q, half):
        if self.by_cols:
            n = self.count if self.z_only else self.count // 4
            first = self.start if self.z_only else self.start + q * n
            rows = pl.ds(first if self.z_only else pl.multiple_of(first, 16), n)
            at, width = core * (self.cols // 2), self.cols // 2
            if half is not None:
                cut = (width // 128 + 1) // 2 * 128
                at, width = (at, cut) if half == 0 else (at + cut, width - cut)
            return rows, pl.ds(pl.multiple_of(at, 128), width)
        n = self.count // 8
        at = self.start + core * (self.count // 2) + q * n
        if half is not None:
            n //= 2
            at = at + half * n
        return pl.ds(pl.multiple_of(at, 16), n), slice(None)

    def mine(self, core, q):
        return self.own.at[self.window(core, q, None)]

    def one(self, d, core, q, half=None):
        return self.others.at[(self.base + d - 1,) + self.window(core, q, half)]

    def all(self, core, q, half=None):
        return self.others.at[(pl.ds(self.base, 3),) + self.window(core, q, half)]


class Gather:
    def __init__(self, chunks, send):
        core, seq, z, y, x = places()
        p = jnp.where(core == 0, x, y)

        def at(k):
            q = (p + k) % 4
            return (core, jnp.where(core == 0, y * 4 + q, q * 4 + x), z)

        self.core, self.p, self.send, self.chunks = core, p, send, chunks
        self.up, self.down = (core, seq, (z + 1) % 4), (core, seq, (z + 3) % 4)
        self.right, self.left, self.other = at(1), at(3), (1 - core, seq, z)
        self.segments = [
            [(int(op[0]), CHUNKS.index(op[1:])) for op in part.split()] for part in PLAN
        ]
        self.state = [{} for _ in chunks]

    def q(self, k):
        return (self.p + k) % 4

    def along(self, i, k, half, peer):
        part = self.chunks[i].all(self.core, self.q(k), half)
        return self.send(part, part, peer)

    def stage0(self, i):
        c = self.chunks[i]
        mine = c.mine(self.core, self.p)
        self.state[i]["z"] = (
            self.send(mine, c.one(1, self.core, self.p), self.down),
            self.send(mine, c.one(3, self.core, self.p), self.up),
        )

    def stage1(self, i):
        c, st = self.chunks[i], self.state[i]
        core, p = self.core, self.p
        st["z"][0].wait_recv()
        low = self.send(c.one(1, core, p, 0), c.one(2, core, p, 0), self.down)
        st["z"][1].wait_recv()
        high = self.send(c.one(3, core, p, 1), c.one(2, core, p, 1), self.up)
        st["far"] = (low, high)

    def stage2(self, i):
        st = self.state[i]
        for copy in st["far"]:
            copy.wait_recv()
        if self.chunks[i].z_only:
            st["last"] = [self.along(i, 0, None, self.other)]
            return
        st["ring"] = (self.along(i, 0, None, self.right), self.along(i, 0, None, self.left))
        st["last"] = [self.along(i, 0, None, self.other)]

    def stage3(self, i):
        st = self.state[i]
        st["ring"][0].wait_recv()
        low = self.along(i, 3, 0, self.right)
        st["last"].append(self.along(i, 3, None, self.other))
        st["ring"][1].wait_recv()
        high = self.along(i, 1, 1, self.left)
        st["last"].append(self.along(i, 1, None, self.other))
        st["ends"] = (low, high)

    def stage4(self, i):
        st = self.state[i]
        for copy in st["ends"]:
            copy.wait_recv()
        st["last"].append(self.along(i, 2, None, self.other))

    def run(self, op):
        stages = (self.stage0, self.stage1, self.stage2, self.stage3, self.stage4)
        if op[0] <= 2 or not self.chunks[op[1]].z_only:
            stages[op[0]](op[1])

    def step(self):
        for op in self.segments.pop(0):
            self.run(op)

    def need(self, i):
        assert not any(at == i for part in self.segments for _, at in part)
        for copy in self.state[i].pop("last", ()):
            copy.wait_recv()

    def end(self):
        while self.segments:
            self.step()
        for i in range(len(self.chunks)):
            self.need(i)


def position_of(sigma):
    return sigma % 64 // 4 * 16 + sigma // 64 * 4 + sigma % 4


def row_order(to_positions):
    a = lax.broadcasted_iota(jnp.int32, (ROWS, ROWS), 0)
    b = lax.broadcasted_iota(jnp.int32, (ROWS, ROWS), 1)
    hit = (position_of(b) == a) if to_positions else (position_of(a) == b)
    return hit.astype(F32).astype(BF)


def normed(values, gain):
    wide = values.astype(F32)
    scale = lax.rsqrt(jnp.mean(wide * wide, axis=-1, keepdims=True) + NORM_EPS)
    return (wide * scale * gain).astype(BF)


def build_spread(spread):
    r = lax.broadcasted_iota(jnp.int32, (128, 256), 0)
    f = lax.broadcasted_iota(jnp.int32, (128, 256), 1)
    i, j = f % 16, (f + f // 16) % 16
    for h in range(QHEADS):
        for side in range(2):
            base = side * 64 + h * 16
            one = (r == base + i) & (f < 160)
            two = (r == base + j) & (f < 144)
            spread[side, 0, :, 256 * h : 256 * (h + 1)] = one.astype(F32).astype(BF)
            spread[side, 1, :, 256 * h : 256 * (h + 1)] = two.astype(F32).astype(BF)


def features(rows, spread, side):
    f = lax.broadcasted_iota(jnp.int32, (1, 256 * QHEADS), 1) % 256
    one = dot(rows, spread[side, 0]) + (f == 160).astype(F32)
    two = dot(rows, spread[side, 1]) + ((f >= 144) & (f <= 160)).astype(F32)
    return one * two


def key_weights():
    f = lax.broadcasted_iota(jnp.int32, (1, 256 * QHEADS), 1) % 256
    pair = jnp.where((f < 16) | (f >= 128), 1.0 / 32, 1.0 / 16)
    return jnp.where(f < 144, pair, jnp.where(f < 160, 0.25, 1.0)).astype(F32)


def local_layer_one(d, x_normed, w_feat, w_val, unpack, spread, nd, phi, state):
    both = dot(x_normed, w_feat).astype(BF)
    queries, keys = both[:, :64], both[:, 64:]
    wide = dot(dot(x_normed, w_val).astype(BF), unpack).astype(BF)
    lane = lax.broadcasted_iota(jnp.int32, (ROWS, 64), 1)
    a = lax.broadcasted_iota(jnp.int32, (ROWS, ROWS), 0)
    b = lax.broadcasted_iota(jnp.int32, (ROWS, ROWS), 1)
    ones = (lax.broadcasted_iota(jnp.int32, (ROWS, 128), 1) == HEAD).astype(F32).astype(BF)
    values = [wide[:, 128 * h : 128 * (h + 1)] + ones for h in range(QHEADS)]
    kernels = []
    for h in range(QHEADS):
        mine = jnp.where(lane // 16 == h, queries, jnp.zeros_like(queries))
        s = dot(mine, keys, ((1,), (1,))) * 0.25
        kernels.append(jnp.where(b <= a, 1.0 + s + 0.5 * s * s, 0.0).astype(BF))
    key_phi = (features(both, spread, 1) * key_weights()).astype(BF)
    phi[d] = features(both, spread, 0).astype(BF)
    for h in range(QHEADS):
        cols = slice(256 * h, 256 * (h + 1))
        state[d * QHEADS + h] = dot(key_phi[:, cols], values[h], ((0,), (0,)))[:STATE].astype(BF)
    for h in range(QHEADS):
        nd[d, :, 128 * h : 128 * (h + 1)] = dot(kernels[h], values[h])


def mix_heads(d, nd, phi, prior, wide):
    full = [
        nd[d, :, 128 * h : 128 * (h + 1)]
        + dot(phi[d, :, 256 * h : 256 * h + STATE], prior[d * QHEADS + h])
        for h in range(QHEADS)
    ]
    for h in range(QHEADS):
        wide[:, 128 * h : 128 * (h + 1)] = (full[h] / full[h][:, HEAD : HEAD + 1]).astype(BF)


def pack_heads():
    a = lax.broadcasted_iota(jnp.int32, (512, 448), 0)
    b = lax.broadcasted_iota(jnp.int32, (512, 448), 1)
    hit = (a // 128 == b // HEAD) & (a % 128 == b % HEAD)
    return hit.astype(F32).astype(BF)


def unpack_heads():
    a = lax.broadcasted_iota(jnp.int32, (448, 512), 0)
    b = lax.broadcasted_iota(jnp.int32, (448, 512), 1)
    hit = (b // 128 == a // HEAD) & (b % 128 == a % HEAD)
    return hit.astype(F32).astype(BF)


def layer_one_kernel(
    wanted, gain, outgoing, feat, val, out_one, win, out_two, taps,
    residual, halo, win_g, out_two_g, taps_g,
    w_feat, w_val, w_out, pages, tokens, arrived, spread, xn, nd, phi, state, blocks, prefix,
    prior, wide, total,
    send_sems, recv_sems, local_sems, page_sems, token_sems, state_sems, prior_sems, halo_sems,
):
    core, seq, z, _, _ = places()
    place = core * 16 + seq
    send = Sender(send_sems, recv_sems)
    chunks = [
        Chunk(feat, w_feat, 1, 0, D, 128, False),
        Chunk(val, w_val, 1, 0, 768, 448, False),
        Chunk(val, w_val, 1, 768, 1024, 448, False),
        Chunk(out_one, w_out, 1, 0, 448, D, True),
        Chunk(win, win_g, 0, 0, 512, 1344, False),
        Chunk(win, win_g, 0, 512, 512, 1344, False),
        Chunk(win, win_g, 0, 1024, 768, 1344, False),
        Chunk(out_two, out_two_g, 0, 0, 448, D, True, True),
    ]
    gather = Gather(chunks, send)

    def copy_to(src, dst, sems, k, peer):
        return pltpu.make_async_remote_copy(
            src_ref=src, dst_ref=dst, send_sem=sems.at[0, k], recv_sem=sems.at[1, k],
            device_id=peer, device_id_type=MESH,
        )

    own = [
        pltpu.make_async_copy(feat, w_feat.at[0], local_sems.at[0]),
        pltpu.make_async_copy(val, w_val.at[0], local_sems.at[1]),
        pltpu.make_async_copy(out_one, w_out.at[0], local_sems.at[2]),
        pltpu.make_async_copy(outgoing.at[place], pages.at[place], local_sems.at[3]),
    ]
    barrier = pltpu.get_barrier_semaphore()
    plane = [((place + k) % 32 // 16, (place + k) % 16, z) for k in range(1, 32)]
    greeted = [(core, seq, (z + k) % 4) for k in (1, 2, 3)] + plane
    for peer in greeted:
        pl.semaphore_signal(barrier, inc=1, device_id=peer, device_id_type=MESH)
    for copy in own:
        copy.start()
    build_spread(spread)
    pl.semaphore_wait(barrier, len(greeted))
    page_copies = [
        copy_to(outgoing.at[(place + k) % 32], pages.at[place], page_sems, k, plane[k - 1])
        for k in range(1, 32)
    ]
    for copy in page_copies:
        copy.start()
    gather.step()
    own[3].wait()
    for copy in page_copies:
        copy.wait_recv()
    column = lax.broadcasted_iota(jnp.int32, (ROWS, ROWS), 1)
    chosen = (wanted[...] == column).astype(F32).astype(BF)
    rows = pages[...].astype(F32).reshape(ROWS, D).astype(BF)
    tokens[...] = dot(chosen, rows).astype(BF).reshape(QUARTERS, 64, D)
    kept = pltpu.make_async_copy(tokens.at[z], arrived.at[z], local_sems.at[3])
    kept.start()
    token_copies = [
        copy_to(tokens.at[(z + k) % 4], arrived.at[z], token_sems, k, (core, seq, (z + k) % 4))
        for k in (1, 2, 3)
    ]
    for copy in token_copies:
        copy.start()
    small = [send(taps, taps_g.at[d - 1], (core, seq, (z + 4 - d) % 4)) for d in (1, 2, 3)]
    gather.step()
    kept.wait()
    for copy in token_copies:
        copy.wait_recv()
    residual[...] = dot(row_order(True), arrived[...].reshape(ROWS, D)).astype(BF)
    xn[...] = normed(residual[...], gain[...])
    gather.step()
    own[0].wait()
    own[1].wait()
    unpack = unpack_heads()

    def state_copy(head, sender):
        return pltpu.make_async_remote_copy(
            src_ref=state.at[head], dst_ref=blocks.at[sender], send_sem=state_sems.at[0, head],
            recv_sem=state_sems.at[1, sender], device_id=(core, head, z), device_id_type=MESH,
        )

    for d in range(QUARTERS):
        if d == 1:
            for i in range(3):
                gather.need(i)
        local_layer_one(d, xn[...], w_feat[d], w_val[d], unpack, spread, nd, phi, state)
        for head in range(d * QHEADS, (d + 1) * QHEADS):

            @pl.when(seq != head)
            def _():
                state_copy(head, seq).start()

        gather.step()
    kept = pltpu.make_async_copy(state.at[seq], blocks.at[seq], local_sems.at[3])
    kept.start()
    gather.step()
    kept.wait()
    for k in range(1, 16):
        state_copy(seq, (seq + k) % 16).wait_recv()
    prefix[0] = jnp.zeros((STATE, 128), BF)

    def add(b, before):
        now = before + blocks[b].astype(F32)
        prefix[b + 1] = now.astype(BF)
        return now

    lax.fori_loop(0, 15, add, jnp.zeros((STATE, 128), F32))
    kept = pltpu.make_async_copy(prefix.at[seq], prior.at[seq], local_sems.at[3])
    kept.start()
    coming = []
    for k in range(1, 16):
        peer = (seq + k) % 16
        coming.append(copy_to(prefix.at[peer], prior.at[seq], prior_sems, k, (core, peer, z)))
    for copy in coming:
        copy.start()
    gather.step()
    pack = pack_heads()
    own[2].wait()
    kept.wait()
    for copy in coming:
        copy.wait_recv()
    for d in range(QUARTERS):
        mix_heads(d, nd, phi, prior, wide)
        mixed = dot(wide[...], pack).astype(BF)
        if d == 1:
            gather.need(3)
        part = dot(mixed, w_out[d]).astype(BF).astype(F32)
        total[...] = part if d == 0 else total[...] + part
        gather.step()
    residual[...] = (residual[...].astype(F32) + total[...]).astype(BF)
    hand_on = copy_to(
        residual.at[pl.ds(ROWS - HALO, HALO)], halo, halo_sems, 0, (core, (seq + 1) % 16, z)
    )
    hand_on.start()
    gather.end()
    hand_on.wait()
    for copy in small:
        copy.wait_recv()
    for copy in page_copies + token_copies + coming + send.copies:
        copy.wait_send()
    for head in range(16):

        @pl.when(seq != head)
        def _():
            state_copy(head, seq).wait_send()


def layer_one(wanted, gain, outgoing, feat, val, out_one, win, out_two, taps):
    heads = QUARTERS * QHEADS
    bulk = 7 * 12 + 5 + 3
    dma = pltpu.SemaphoreType.DMA
    return pl.pallas_call(
        layer_one_kernel,
        out_shape=[
            jax.ShapeDtypeStruct((ROWS, D), BF),
            jax.ShapeDtypeStruct((HALO, D), BF),
            jax.ShapeDtypeStruct((3, D, 1344), BF),
            jax.ShapeDtypeStruct((3, 448, D), BF),
            jax.ShapeDtypeStruct((3, 3, 3, 448), F32),
        ],
        in_specs=[VM, VM] + [ANY] * 7,
        out_specs=[VM, VM] + [ANY] * 3,
        scratch_shapes=[
            pltpu.VMEM((QUARTERS, D, 128), BF),
            pltpu.VMEM((QUARTERS, D, 448), BF),
            pltpu.VMEM((QUARTERS, 448, D), BF),
            pltpu.VMEM((32, 8, D), BF),
            pltpu.VMEM((QUARTERS, 64, D), BF),
            pltpu.VMEM((QUARTERS, 64, D), BF),
            pltpu.VMEM((2, 2, 128, 256 * QHEADS), BF),
            pltpu.VMEM((ROWS, D), BF),
            pltpu.VMEM((QUARTERS, ROWS, 512), F32),
            pltpu.VMEM((QUARTERS, ROWS, 1024), BF),
            pltpu.VMEM((heads, STATE, 128), BF),
            pltpu.VMEM((16, STATE, 128), BF),
            pltpu.VMEM((16, STATE, 128), BF),
            pltpu.VMEM((heads, STATE, 128), BF),
            pltpu.VMEM((ROWS, 512), BF),
            pltpu.VMEM((ROWS, D), F32),
            dma((bulk,)),
            dma((bulk,)),
            dma((4,)),
            dma((2, 32)),
            dma((2, 4)),
            dma((2, 16)),
            dma((2, 16)),
            dma((2, 1)),
        ],
        compiler_params=pltpu.CompilerParams(
            collective_id=0, has_side_effects=True, vmem_limit_bytes=52 << 20
        ),
        name="layer_one",
    )(wanted, gain, outgoing, feat, val, out_one, win, out_two, taps)


def layer_two_quarter(first_block, xn, weight, taps, unpack, qkv, wide):
    span = ROWS + WINDOW
    for part in range(3):
        cols = slice(448 * part, 448 * (part + 1))
        projected = dot(xn, weight[:, cols])
        conv = taps[0, part : part + 1] * projected[HALO - WINDOW :]
        for j in (1, 2):
            conv = conv + taps[j, part : part + 1] * projected[HALO - WINDOW - j : HALO + ROWS - j]
        qkv[part] = dot(conv.astype(BF), unpack).astype(BF)
    q_at = lax.broadcasted_iota(jnp.int32, (64, 128), 0)
    k_at = lax.broadcasted_iota(jnp.int32, (64, 128), 1) - WINDOW
    band = (k_at <= q_at) & (k_at > q_at - WINDOW)
    inside = band & ((k_at >= 0) | jnp.logical_not(first_block))
    tiles = [(h, 64 * t) for h in range(QHEADS) for t in range(4)]
    logits = []
    for h, at in tiles:
        lanes = slice(128 * h, 128 * (h + 1))
        q = qkv[0, WINDOW + at : WINDOW + at + 64, lanes]
        k = qkv[1, at : at + 128, lanes]
        scaled = dot(q, k, ((1,), (1,))) * HEAD ** (-0.5)
        logits.append(jnp.where(band if at else inside, scaled, -jnp.inf))
    logits = jnp.concatenate(logits, axis=0)
    weights = jnp.exp(logits - jnp.max(logits, axis=1, keepdims=True))
    attention = (weights / jnp.sum(weights, axis=1, keepdims=True)).astype(BF)
    for n, (h, at) in enumerate(tiles):
        lanes = slice(128 * h, 128 * (h + 1))
        v = qkv[2, at : at + 128, lanes]
        wide[at : at + 64, lanes] = dot(attention[64 * n : 64 * (n + 1)], v).astype(BF)


def layer_two_kernel(
    live, residual, halo, gain, taps, taps_others, win, win_others, wout, wout_others, out,
    weights, weights_out, xn, qkv, wide, total, result_rows, sems, out_sems,
):
    def pair(own, others, buf, k0):
        return [pltpu.make_async_copy(own, buf.at[0], sems.at[k0])] + [
            pltpu.make_async_copy(others.at[k], buf.at[k + 1], sems.at[k0 + k + 1])
            for k in range(3)
        ]

    first_copies = pair(win, win_others, weights, 0)
    second_copies = pair(wout, wout_others, weights_out, 4)
    for a, b in zip(first_copies, second_copies):
        a.start()
        b.start()
    core, seq, z, _, _ = places()
    peers = [(core, seq, (z + k) % 4) for k in (2, 1, 3)]
    barrier = pltpu.get_barrier_semaphore()
    for peer in peers:
        pl.semaphore_signal(barrier, inc=1, device_id=peer, device_id_type=MESH)
    first_block = seq == 0
    before = halo[...]
    xn[:HALO] = normed(jnp.where(first_block, jnp.zeros_like(before), before), gain[...])
    xn[HALO:] = normed(residual[...], gain[...])
    pack, unpack = pack_heads(), unpack_heads()
    for d in range(QUARTERS):
        tap = taps[...] if d == 0 else taps_others[d - 1]
        first_copies[d].wait()
        layer_two_quarter(first_block, xn[...], weights.at[d], tap, unpack, qkv, wide)
        mixed = dot(wide[...], pack).astype(BF)
        second_copies[d].wait()
        part = dot(mixed, weights_out[d]).astype(BF).astype(F32)
        total[...] = part if d == 0 else total[...] + part
    row = lax.broadcasted_iota(jnp.int32, (ROWS, 1), 0) + seq * ROWS
    result = (residual[...].astype(F32) + total[...]).astype(BF)
    result = jnp.where(row < live[core * 4 + z], result, jnp.zeros_like(result))
    result_rows[...] = dot(row_order(False), result).astype(BF).reshape(QUARTERS, 64, D)
    pl.semaphore_wait(barrier, 3)
    kept = pltpu.make_async_copy(result_rows.at[z], out.at[z], sems.at[0])
    kept.start()
    copies = []
    for n, k in enumerate((2, 1, 3)):
        copy = pltpu.make_async_remote_copy(
            src_ref=result_rows.at[(z + k) % 4], dst_ref=out.at[z], send_sem=out_sems.at[0, n],
            recv_sem=out_sems.at[1, n], device_id=peers[n], device_id_type=MESH,
        )
        copy.start()
        copies.append(copy)
    kept.wait()
    for copy in copies:
        copy.wait()


def layer_two(live, residual, halo, gain, taps, taps_others, win, win_others, wout, wout_others):
    return pl.pallas_call(
        layer_two_kernel,
        out_shape=jax.ShapeDtypeStruct((QUARTERS, 64, D), BF),
        in_specs=[pl.BlockSpec(memory_space=pltpu.SMEM)] + [VM] * 5 + [ANY] * 4,
        out_specs=ANY,
        scratch_shapes=[
            pltpu.VMEM((QUARTERS, D, 1344), BF),
            pltpu.VMEM((QUARTERS, 448, D), BF),
            pltpu.VMEM((ROWS + HALO, D), BF),
            pltpu.VMEM((3, ROWS + WINDOW, 512), BF),
            pltpu.VMEM((ROWS, 512), BF),
            pltpu.VMEM((ROWS, D), F32),
            pltpu.VMEM((QUARTERS, 64, D), BF),
            pltpu.SemaphoreType.DMA((8,)),
            pltpu.SemaphoreType.DMA((2, 3)),
        ],
        compiler_params=pltpu.CompilerParams(
            collective_id=1, has_side_effects=True, vmem_limit_bytes=60 << 20
        ),
        name="layer_two",
    )(live, residual, halo, gain, taps, taps_others, win, win_others, wout, wout_others)


def on_device(
    pool, page_table, reassign, lengths, gain_one, w_featmap, w_value, w_out_one,
    gain_two, w_window, conv_window, w_out_two,
):
    groups = 32
    device_place = lax.axis_index(("dp", "seq"))
    seq, core, z = lax.axis_index("seq"), lax.axis_index("dp"), lax.axis_index("tensor")
    pages_dev, page_share = pool.shape[:2]
    table = page_table[reassign]
    source = table.reshape(2, 4, 16, 16).transpose(0, 2, 1, 3).reshape(groups, pages_dev)
    owner, slot_of = source // pages_dev, source % pages_dev
    before = jnp.arange(pages_dev)[None, :] < jnp.arange(pages_dev)[:, None]
    rank = jnp.sum((owner[:, :, None] == owner[:, None, :]) & before[None], axis=2)
    hit = (owner == device_place)[:, None, :] & (rank[:, None, :] == jnp.arange(2)[None, :, None])
    send_slot = jnp.sum(jnp.where(hit, slot_of[:, None, :], 0), axis=2)
    outgoing = jnp.take(pool, send_slot.reshape(-1), axis=0).reshape(groups, 8, D)
    row_hit = (jnp.arange(groups) == device_place)[:, None]
    pick = jnp.sum(jnp.where(row_hit, owner * 2 + rank, 0), axis=0)
    wanted = (pick[:, None] * 4 + jnp.arange(4)[None, :]).reshape(ROWS, 1)
    feat = w_featmap.reshape(D, 128)
    win = w_window.reshape(D, 1344)
    residual, halo, win_g, out_two_g, taps_g = layer_one(
        wanted, gain_one[None], outgoing, feat, w_value, w_out_one, win, w_out_two, conv_window
    )
    live = lengths[reassign]
    result = layer_two(
        live, residual, halo, gain_two[None], conv_window, taps_g, win, win_g, w_out_two, out_two_g
    )
    return result.reshape(4, 16, 4, D)


def solution(mesh):
    return jax.shard_map(
        on_device,
        mesh=mesh,
        in_specs=(
            P(("dp", "seq"), "tensor", None),
            P(),
            P(),
            P(),
            P(),
            P(None, None, "tensor"),
            P(None, "tensor"),
            P("tensor", None),
            P(),
            P(None, None, "tensor"),
            P(None, None, "tensor"),
            P("tensor", None),
        ),
        out_specs=P("dp", "seq", "tensor", None),
        check_vma=False,
    )
```

```python
import functools

import jax
import jax.numpy as jnp
from jax import lax
from jax.experimental import pallas as pl
from jax.experimental.pallas import tpu as pltpu
from jax.sharding import PartitionSpec as P

HEAD = 112
FEAT = 16
WINDOW = 64
D = 1792
ROWS = 256
HALO = 80
QUARTERS = 4
QHEADS = 4
STATE = 176
CHUNKS = ["f", "v0", "v1", "o", "w0", "w1", "w2", "p"]
PLAN = (
    "0f 0v0 0v1 1f 1v0 1v1 2f 2v0 2v1",
    "0o 3f 3v0 3v1",
    "",
    "4f 4v0 4v1 1o 0w0 2o",
    "1w0 0w1",
    "2w0",
    "3o 1w1 0w2",
    "2w1 4o",
    "3w0 1w2 0p",
    "2w2",
    "3w1 4w0",
    "1p",
    "3w2 4w1",
    "4w2 2p",
)
NORM_EPS = 1e-05
MESH = pl.DeviceIdType.MESH
BF = jnp.bfloat16
F32 = jnp.float32
ANY = pl.BlockSpec(memory_space=pl.ANY)
VM = pl.BlockSpec(memory_space=pltpu.VMEM)


def dot(a, b, dims=((1,), (0,))):
    return lax.dot_general(a, b, (dims, ((), ())), preferred_element_type=F32)


def places():
    core, seq, z = lax.axis_index("dp"), lax.axis_index("seq"), lax.axis_index("tensor")
    return core, seq, z, seq // 4, seq % 4


class Sender:
    def __init__(self, send_sems, recv_sems):
        self.send_sems, self.recv_sems, self.copies = send_sems, recv_sems, []

    def __call__(self, src, dst, peer):
        k = len(self.copies)
        copy = pltpu.make_async_remote_copy(
            src_ref=src,
            dst_ref=dst,
            send_sem=self.send_sems.at[k],
            recv_sem=self.recv_sems.at[k],
            device_id=peer,
            device_id_type=MESH,
        )
        copy.start()
        self.copies.append(copy)
        return copy


class Chunk:
    def __init__(self, own, others, start, count, z_only=False):
        self.own, self.others, self.start, self.count = own, others, start, count
        self.z_only = z_only

    def window(self, core, q, half):
        n = self.count if self.z_only else self.count // 4
        rows = pl.ds(self.start if self.z_only else pl.multiple_of(self.start + q * n, 16), n)
        at, width = core * (D // 2), D // 2
        if half is not None:
            cut = (width // 128 + 1) // 2 * 128
            at, width = (at, cut) if half == 0 else (at + cut, width - cut)
        return rows, pl.ds(pl.multiple_of(at, 128), width)

    def mine(self, core, q):
        return self.own.at[self.window(core, q, None)]

    def one(self, d, core, q, half=None):
        return self.others.at[(d,) + self.window(core, q, half)]

    def all(self, core, q, half=None):
        return self.others.at[(pl.ds(1, 3),) + self.window(core, q, half)]


class Gather:
    def __init__(self, chunks, send):
        core, seq, z, y, x = places()
        p = jnp.where(core == 0, x, y)

        def at(k):
            q = (p + k) % 4
            return (core, jnp.where(core == 0, y * 4 + q, q * 4 + x), z)

        self.core, self.p, self.send, self.chunks = core, p, send, chunks
        self.up, self.down = (core, seq, (z + 1) % 4), (core, seq, (z + 3) % 4)
        self.right, self.left, self.other = at(1), at(3), (1 - core, seq, z)
        self.segments = [
            [(int(op[0]), CHUNKS.index(op[1:])) for op in part.split()] for part in PLAN
        ]
        self.state = [{} for _ in chunks]

    def q(self, k):
        return (self.p + k) % 4

    def along(self, i, k, half, peer):
        part = self.chunks[i].all(self.core, self.q(k), half)
        return self.send(part, part, peer)

    def stage0(self, i):
        c = self.chunks[i]
        mine = c.mine(self.core, self.p)
        self.state[i]["z"] = (
            self.send(mine, c.one(1, self.core, self.p), self.down),
            self.send(mine, c.one(3, self.core, self.p), self.up),
        )

    def stage1(self, i):
        c, st = self.chunks[i], self.state[i]
        core, p = self.core, self.p
        st["z"][0].wait_recv()
        low = self.send(c.one(1, core, p, 0), c.one(2, core, p, 0), self.down)
        st["z"][1].wait_recv()
        high = self.send(c.one(3, core, p, 1), c.one(2, core, p, 1), self.up)
        st["far"] = (low, high)

    def stage2(self, i):
        st = self.state[i]
        for copy in st["far"]:
            copy.wait_recv()
        if self.chunks[i].z_only:
            st["last"] = [self.along(i, 0, None, self.other)]
            return
        st["ring"] = (self.along(i, 0, None, self.right), self.along(i, 0, None, self.left))
        st["last"] = [self.along(i, 0, None, self.other)]

    def stage3(self, i):
        st = self.state[i]
        st["ring"][0].wait_recv()
        low = self.along(i, 3, 0, self.right)
        st["last"].append(self.along(i, 3, None, self.other))
        st["ring"][1].wait_recv()
        high = self.along(i, 1, 1, self.left)
        st["last"].append(self.along(i, 1, None, self.other))
        st["ends"] = (low, high)

    def stage4(self, i):
        st = self.state[i]
        for copy in st["ends"]:
            copy.wait_recv()
        st["last"].append(self.along(i, 2, None, self.other))

    def run(self, op):
        stages = (self.stage0, self.stage1, self.stage2, self.stage3, self.stage4)
        if op[0] <= 2 or not self.chunks[op[1]].z_only:
            stages[op[0]](op[1])

    def step(self):
        for op in self.segments.pop(0):
            self.run(op)

    def need(self, i):
        assert not any(at == i for part in self.segments for _, at in part)
        for copy in self.state[i].pop("last", ()):
            copy.wait_recv()

    def end(self):
        while self.segments:
            self.step()
        for i in range(len(self.chunks)):
            self.need(i)


def position_of(sigma):
    return sigma % 64 // 4 * 16 + sigma // 64 * 4 + sigma % 4


def row_order(to_positions):
    a = lax.broadcasted_iota(jnp.int32, (ROWS, ROWS), 0)
    b = lax.broadcasted_iota(jnp.int32, (ROWS, ROWS), 1)
    hit = (position_of(b) == a) if to_positions else (position_of(a) == b)
    return hit.astype(F32).astype(BF)


def normed(values, gain):
    wide = values.astype(F32)
    scale = lax.rsqrt(jnp.mean(wide * wide, axis=-1, keepdims=True) + NORM_EPS)
    return (wide * scale * gain).astype(BF)


def build_spread(spread):
    r = lax.broadcasted_iota(jnp.int32, (128, 256), 0)
    f = lax.broadcasted_iota(jnp.int32, (128, 256), 1)
    i, j = f % 16, (f + f // 16) % 16
    for h in range(QHEADS):
        for side in range(2):
            base = side * 64 + h * 16
            one = (r == base + i) & (f < 160)
            two = (r == base + j) & (f < 144)
            spread[side, 0, :, 256 * h : 256 * (h + 1)] = one.astype(F32).astype(BF)
            spread[side, 1, :, 256 * h : 256 * (h + 1)] = two.astype(F32).astype(BF)


def features(rows, spread, side):
    f = lax.broadcasted_iota(jnp.int32, (1, 256 * QHEADS), 1) % 256
    one = dot(rows, spread[side, 0]) + (f == 160).astype(F32)
    two = dot(rows, spread[side, 1]) + ((f >= 144) & (f <= 160)).astype(F32)
    return one * two


def key_weights():
    f = lax.broadcasted_iota(jnp.int32, (1, 256 * QHEADS), 1) % 256
    pair = jnp.where((f < 16) | (f >= 128), 1.0 / 32, 1.0 / 16)
    return jnp.where(f < 144, pair, jnp.where(f < 160, 0.25, 1.0)).astype(F32)


def local_layer_one(d, x_normed, w_feat, w_val, unpack, spread, nd, phi, state):
    both = dot(x_normed, w_feat, ((1,), (1,))).astype(BF)
    queries, keys = both[:, :64], both[:, 64:]
    wide = dot(dot(x_normed, w_val, ((1,), (1,))).astype(BF), unpack).astype(BF)
    lane = lax.broadcasted_iota(jnp.int32, (ROWS, 64), 1)
    a = lax.broadcasted_iota(jnp.int32, (ROWS, ROWS), 0)
    b = lax.broadcasted_iota(jnp.int32, (ROWS, ROWS), 1)
    ones = (lax.broadcasted_iota(jnp.int32, (ROWS, 128), 1) == HEAD).astype(F32).astype(BF)
    values = [wide[:, 128 * h : 128 * (h + 1)] + ones for h in range(QHEADS)]
    kernels = []
    for h in range(QHEADS):
        mine = jnp.where(lane // 16 == h, queries, jnp.zeros_like(queries))
        s = dot(mine, keys, ((1,), (1,))) * 0.25
        kernels.append(jnp.where(b <= a, 1.0 + s + 0.5 * s * s, 0.0).astype(BF))
    key_phi = (features(both, spread, 1) * key_weights()).astype(BF)
    phi[d] = features(both, spread, 0).astype(BF)
    for h in range(QHEADS):
        cols = slice(256 * h, 256 * (h + 1))
        state[d * QHEADS + h] = dot(key_phi[:, cols], values[h], ((0,), (0,)))[:STATE].astype(BF)
    for h in range(QHEADS):
        nd[d, :, 128 * h : 128 * (h + 1)] = dot(kernels[h], values[h])


def mix_heads(d, nd, phi, prior, wide):
    full = [
        nd[d, :, 128 * h : 128 * (h + 1)]
        + dot(phi[d, :, 256 * h : 256 * h + STATE], prior[d * QHEADS + h])
        for h in range(QHEADS)
    ]
    for h in range(QHEADS):
        wide[:, 128 * h : 128 * (h + 1)] = (full[h] / full[h][:, HEAD : HEAD + 1]).astype(BF)


def pack_heads():
    a = lax.broadcasted_iota(jnp.int32, (512, 448), 0)
    b = lax.broadcasted_iota(jnp.int32, (512, 448), 1)
    hit = (a // 128 == b // HEAD) & (a % 128 == b % HEAD)
    return hit.astype(F32).astype(BF)


def unpack_heads():
    a = lax.broadcasted_iota(jnp.int32, (448, 512), 0)
    b = lax.broadcasted_iota(jnp.int32, (448, 512), 1)
    hit = (b // 128 == a // HEAD) & (b % 128 == a % HEAD)
    return hit.astype(F32).astype(BF)


def layer_two_quarter(first_block, xn, weight, taps, unpack, qkv, wide):
    span = ROWS + WINDOW
    for part in range(3):
        projected = dot(xn, weight[448 * part : 448 * (part + 1)], ((1,), (1,)))
        conv = taps[0, part : part + 1] * projected[HALO - WINDOW :]
        for j in (1, 2):
            conv = conv + taps[j, part : part + 1] * projected[HALO - WINDOW - j : HALO + ROWS - j]
        qkv[part] = dot(conv.astype(BF), unpack).astype(BF)
    q_at = lax.broadcasted_iota(jnp.int32, (64, 128), 0)
    k_at = lax.broadcasted_iota(jnp.int32, (64, 128), 1) - WINDOW
    band = (k_at <= q_at) & (k_at > q_at - WINDOW)
    inside = band & ((k_at >= 0) | jnp.logical_not(first_block))
    tiles = [(h, 64 * t) for h in range(QHEADS) for t in range(4)]
    logits = []
    for h, at in tiles:
        lanes = slice(128 * h, 128 * (h + 1))
        q = qkv[0, WINDOW + at : WINDOW + at + 64, lanes]
        k = qkv[1, at : at + 128, lanes]
        scaled = dot(q, k, ((1,), (1,))) * HEAD ** (-0.5)
        logits.append(jnp.where(band if at else inside, scaled, -jnp.inf))
    logits = jnp.concatenate(logits, axis=0)
    weights = jnp.exp(logits - jnp.max(logits, axis=1, keepdims=True))
    attention = (weights / jnp.sum(weights, axis=1, keepdims=True)).astype(BF)
    for n, (h, at) in enumerate(tiles):
        lanes = slice(128 * h, 128 * (h + 1))
        v = qkv[2, at : at + 128, lanes]
        wide[at : at + 64, lanes] = dot(attention[64 * n : 64 * (n + 1)], v).astype(BF)


def layers_kernel(
    live, wanted, gain, gain_two, outgoing, feat, val, out_one, win, out_two, taps,
    out,
    w_feat, w_val, w_out, w_win, w_two, w_taps, pages, tokens, arrived, spread, xn, nd, phi,
    state, blocks, prefix, prior, wide, total, residual, halo, qkv,
    send_sems, recv_sems, local_sems, page_sems, token_sems, state_sems, prior_sems, halo_sems, out_sems,
):
    core, seq, z, _, _ = places()
    place = core * 16 + seq
    send = Sender(send_sems, recv_sems)
    chunks = [
        Chunk(feat, w_feat, 0, 128),
        Chunk(val, w_val, 0, 192),
        Chunk(val, w_val, 192, 256),
        Chunk(out_one, w_out, 0, 448),
        Chunk(win, w_win, 0, 448),
        Chunk(win, w_win, 448, 448),
        Chunk(win, w_win, 896, 448),
        Chunk(out_two, w_two, 0, 448, True),
    ]
    gather = Gather(chunks, send)
    first_block = seq == 0

    def copy_to(src, dst, sems, k, peer):
        return pltpu.make_async_remote_copy(
            src_ref=src, dst_ref=dst, send_sem=sems.at[0, k], recv_sem=sems.at[1, k],
            device_id=peer, device_id_type=MESH,
        )

    own = [
        pltpu.make_async_copy(feat, w_feat.at[0], local_sems.at[0]),
        pltpu.make_async_copy(val, w_val.at[0], local_sems.at[1]),
        pltpu.make_async_copy(out_one, w_out.at[0], local_sems.at[2]),
        pltpu.make_async_copy(outgoing.at[place], pages.at[place], local_sems.at[3]),
        pltpu.make_async_copy(win, w_win.at[0], local_sems.at[4]),
        pltpu.make_async_copy(out_two, w_two.at[0], local_sems.at[5]),
        pltpu.make_async_copy(taps, w_taps.at[0], local_sems.at[6]),
    ]
    barrier = pltpu.get_barrier_semaphore()
    plane = [((place + k) % 32 // 16, (place + k) % 16, z) for k in range(1, 32)]
    greeted = [(core, seq, (z + k) % 4) for k in (1, 2, 3)] + plane
    for peer in greeted:
        pl.semaphore_signal(barrier, inc=1, device_id=peer, device_id_type=MESH)
    for copy in own:
        copy.start()
    build_spread(spread)
    pl.semaphore_wait(barrier, len(greeted))
    page_copies = [
        copy_to(outgoing.at[(place + k) % 32], pages.at[place], page_sems, k, plane[k - 1])
        for k in range(1, 32)
    ]
    for copy in page_copies:
        copy.start()
    gather.step()
    own[3].wait()
    for copy in page_copies:
        copy.wait_recv()
    column = lax.broadcasted_iota(jnp.int32, (ROWS, ROWS), 1)
    chosen = (wanted[...] == column).astype(F32).astype(BF)
    rows = pages[...].astype(F32).reshape(ROWS, D).astype(BF)
    tokens[...] = dot(chosen, rows).astype(BF).reshape(QUARTERS, 64, D)
    kept = pltpu.make_async_copy(tokens.at[z], arrived.at[z], local_sems.at[3])
    kept.start()
    token_copies = [
        copy_to(tokens.at[(z + k) % 4], arrived.at[z], token_sems, k, (core, seq, (z + k) % 4))
        for k in (1, 2, 3)
    ]
    for copy in token_copies:
        copy.start()
    small = [send(taps, w_taps.at[d], (core, seq, (z + 4 - d) % 4)) for d in (1, 2, 3)]
    gather.step()
    kept.wait()
    for copy in token_copies:
        copy.wait_recv()
    residual[...] = dot(row_order(True), arrived[...].reshape(ROWS, D)).astype(BF)
    xn[HALO:] = normed(residual[...], gain[...].reshape(1, D))
    gather.step()
    own[0].wait()
    own[1].wait()
    unpack = unpack_heads()

    def state_copy(head, sender):
        return pltpu.make_async_remote_copy(
            src_ref=state.at[head], dst_ref=blocks.at[sender], send_sem=state_sems.at[0, head],
            recv_sem=state_sems.at[1, sender], device_id=(core, head, z), device_id_type=MESH,
        )

    for d in range(QUARTERS):
        if d == 1:
            for i in range(3):
                gather.need(i)
        local_layer_one(d, xn[HALO:], w_feat[d], w_val[d], unpack, spread, nd, phi, state)
        for head in range(d * QHEADS, (d + 1) * QHEADS):

            @pl.when(seq != head)
            def _():
                state_copy(head, seq).start()

        gather.step()
    kept = pltpu.make_async_copy(state.at[seq], blocks.at[seq], local_sems.at[3])
    kept.start()
    gather.step()
    kept.wait()
    for k in range(1, 16):
        state_copy(seq, (seq + k) % 16).wait_recv()
    prefix[0] = jnp.zeros((STATE, 128), BF)

    def add(b, before):
        now = before + blocks[b].astype(F32)
        prefix[b + 1] = now.astype(BF)
        return now

    lax.fori_loop(0, 15, add, jnp.zeros((STATE, 128), F32))
    kept = pltpu.make_async_copy(prefix.at[seq], prior.at[seq], local_sems.at[3])
    kept.start()
    coming = []
    for k in range(1, 16):
        peer = (seq + k) % 16
        coming.append(copy_to(prefix.at[peer], prior.at[seq], prior_sems, k, (core, peer, z)))
    for copy in coming:
        copy.start()
    gather.step()
    pack = pack_heads()
    own[2].wait()
    kept.wait()
    for copy in coming:
        copy.wait_recv()
    for d in range(QUARTERS):
        mix_heads(d, nd, phi, prior, wide)
        mixed = dot(wide[...], pack).astype(BF)
        if d == 1:
            gather.need(3)
        part = dot(mixed, w_out[d]).astype(BF).astype(F32)
        total[...] = part if d == 0 else total[...] + part
        gather.step()
    residual[...] = (residual[...].astype(F32) + total[...]).astype(BF)
    hand_on = copy_to(
        residual.at[pl.ds(ROWS - HALO, HALO)], halo, halo_sems, 0, (core, (seq + 1) % 16, z)
    )
    hand_on.start()
    xn[HALO:] = normed(residual[...], gain_two[...].reshape(1, D))
    gather.step()
    hand_on.wait_recv()
    before = halo[...]
    xn[:HALO] = normed(jnp.where(first_block, jnp.zeros_like(before), before), gain_two[...].reshape(1, D))
    for copy in own[4:]:
        copy.wait()
    for d in range(QUARTERS):
        if d == 1:
            gather.end()
            for copy in small:
                copy.wait_recv()
        layer_two_quarter(
            first_block, xn[...], w_win.at[d], w_taps.at[d], unpack, qkv, wide
        )
        mixed = dot(wide[...], pack).astype(BF)
        part = dot(mixed, w_two[d]).astype(BF).astype(F32)
        total[...] = part if d == 0 else total[...] + part
    row = lax.broadcasted_iota(jnp.int32, (ROWS, 1), 0) + seq * ROWS
    result = (residual[...].astype(F32) + total[...]).astype(BF)
    result = jnp.where(row < live[core * 4 + z], result, jnp.zeros_like(result))
    for copy in token_copies:
        copy.wait_send()
    tokens[...] = dot(row_order(False), result).astype(BF).reshape(QUARTERS, 64, D)
    kept = pltpu.make_async_copy(tokens.at[z], out.at[z], local_sems.at[3])
    kept.start()
    finals = [
        copy_to(tokens.at[(z + k) % 4], out.at[z], out_sems, k, (core, seq, (z + k) % 4))
        for k in (2, 1, 3)
    ]
    for copy in finals:
        copy.start()
    kept.wait()
    for copy in finals:
        copy.wait()
    hand_on.wait_send()
    for copy in page_copies + coming + send.copies:
        copy.wait_send()
    for head in range(16):

        @pl.when(seq != head)
        def _():
            state_copy(head, seq).wait_send()


def layers(live, *arrays):
    heads = QUARTERS * QHEADS
    bulk = 7 * 12 + 5 + 3
    dma = pltpu.SemaphoreType.DMA
    return pl.pallas_call(
        layers_kernel,
        out_shape=jax.ShapeDtypeStruct((QUARTERS, 64, D), BF),
        in_specs=[pl.BlockSpec(memory_space=pltpu.SMEM)] + [VM] * 3 + [ANY] * 7,
        out_specs=ANY,
        scratch_shapes=[
            pltpu.VMEM((QUARTERS, 128, D), BF),
            pltpu.VMEM((QUARTERS, 448, D), BF),
            pltpu.VMEM((QUARTERS, 448, D), BF),
            pltpu.VMEM((QUARTERS, 1344, D), BF),
            pltpu.VMEM((QUARTERS, 448, D), BF),
            pltpu.VMEM((QUARTERS, 3, 3, 448), F32),
            pltpu.VMEM((32, 8, D), BF),
            pltpu.VMEM((QUARTERS, 64, D), BF),
            pltpu.VMEM((QUARTERS, 64, D), BF),
            pltpu.VMEM((2, 2, 128, 256 * QHEADS), BF),
            pltpu.VMEM((ROWS + HALO, D), BF),
            pltpu.VMEM((QUARTERS, ROWS, 512), F32),
            pltpu.VMEM((QUARTERS, ROWS, 1024), BF),
            pltpu.VMEM((heads, STATE, 128), BF),
            pltpu.VMEM((16, STATE, 128), BF),
            pltpu.VMEM((16, STATE, 128), BF),
            pltpu.VMEM((heads, STATE, 128), BF),
            pltpu.VMEM((ROWS, 512), BF),
            pltpu.VMEM((ROWS, D), F32),
            pltpu.VMEM((ROWS, D), BF),
            pltpu.VMEM((HALO, D), BF),
            pltpu.VMEM((3, ROWS + WINDOW, 512), BF),
            dma((bulk,)),
            dma((bulk,)),
            dma((7,)),
            dma((2, 32)),
            dma((2, 4)),
            dma((2, 16)),
            dma((2, 16)),
            dma((2, 1)),
            dma((2, 4)),
        ],
        compiler_params=pltpu.CompilerParams(
            collective_id=0, has_side_effects=True, vmem_limit_bytes=63 << 20
        ),
        name="layers",
    )(live, *arrays)


def on_device(
    pool, page_table, reassign, lengths, gain_one, w_featmap, w_value, w_out_one,
    gain_two, w_window, conv_window, w_out_two,
):
    groups = 32
    device_place = lax.axis_index(("dp", "seq"))
    seq, core, z = lax.axis_index("seq"), lax.axis_index("dp"), lax.axis_index("tensor")
    pages_dev, page_share = pool.shape[:2]
    table = page_table[reassign]
    source = table.reshape(2, 4, 16, 16).transpose(0, 2, 1, 3).reshape(groups, pages_dev)
    owner, slot_of = source // pages_dev, source % pages_dev
    before = jnp.arange(pages_dev)[None, :] < jnp.arange(pages_dev)[:, None]
    rank = jnp.sum((owner[:, :, None] == owner[:, None, :]) & before[None], axis=2)
    hit = (owner == device_place)[:, None, :] & (rank[:, None, :] == jnp.arange(2)[None, :, None])
    send_slot = jnp.sum(jnp.where(hit, slot_of[:, None, :], 0), axis=2)
    outgoing = jnp.take(pool, send_slot.reshape(-1), axis=0).reshape(groups, 8, D)
    row_hit = (jnp.arange(groups) == device_place)[:, None]
    pick = jnp.sum(jnp.where(row_hit, owner * 2 + rank, 0), axis=0)
    wanted = (pick[:, None] * 4 + jnp.arange(4)[None, :]).reshape(ROWS, 1)
    feat = w_featmap.transpose(1, 2, 0).reshape(128, D)
    win = w_window.transpose(1, 2, 0).reshape(1344, D)
    result = layers(
        lengths[reassign], wanted, gain_one, gain_two, outgoing, feat, w_value.T,
        w_out_one, win, w_out_two, conv_window,
    )
    return result.reshape(4, 16, 4, D)


def solution(mesh):
    return jax.shard_map(
        on_device,
        mesh=mesh,
        in_specs=(
            P(("dp", "seq"), "tensor", None),
            P(),
            P(),
            P(),
            P(),
            P(None, None, "tensor"),
            P(None, "tensor"),
            P("tensor", None),
            P(),
            P(None, None, "tensor"),
            P(None, None, "tensor"),
            P("tensor", None),
        ),
        out_specs=P("dp", "seq", "tensor", None),
        check_vma=False,
    )
```

```python
import functools

import jax
import jax.numpy as jnp
from jax import lax
from jax.experimental import pallas as pl
from jax.experimental.pallas import tpu as pltpu
from jax.sharding import PartitionSpec as P

HEAD = 112
FEAT = 16
WINDOW = 64
D = 1792
ROWS = 256
HALO = 80
QUARTERS = 4
QHEADS = 4
STATE = 176
CHUNKS = ["f", "v0", "v1", "o", "w0", "w1", "w2", "p"]
PLAN = (
    "0f 0v0 0v1 1f 1v0 1v1 2f 2v0 2v1",
    "0o 3f 3v0 3v1",
    "",
    "4f 4v0 4v1 1o 0w0 2o",
    "1w0 0w1",
    "2w0 0w2",
    "3o 1w1 0p",
    "2w1 4o",
    "3w0 1w2",
    "2w2",
    "3w1 4w0",
    "1p",
    "",
    "3w2 4w1",
    "4w2 2p",
)
NORM_EPS = 1e-05
MESH = pl.DeviceIdType.MESH
BF = jnp.bfloat16
F32 = jnp.float32
ANY = pl.BlockSpec(memory_space=pl.ANY)
VM = pl.BlockSpec(memory_space=pltpu.VMEM)


def dot(a, b, dims=((1,), (0,))):
    return lax.dot_general(a, b, (dims, ((), ())), preferred_element_type=F32)


def places():
    core, seq, z = lax.axis_index("dp"), lax.axis_index("seq"), lax.axis_index("tensor")
    return core, seq, z, seq // 4, seq % 4


class Sender:
    def __init__(self, send_sems, recv_sems):
        self.send_sems, self.recv_sems, self.copies = send_sems, recv_sems, []

    def __call__(self, src, dst, peer):
        k = len(self.copies)
        copy = pltpu.make_async_remote_copy(
            src_ref=src,
            dst_ref=dst,
            send_sem=self.send_sems.at[k],
            recv_sem=self.recv_sems.at[k],
            device_id=peer,
            device_id_type=MESH,
        )
        copy.start()
        self.copies.append(copy)
        return copy


class Chunk:
    def __init__(self, own, others, start, count, z_only=False):
        self.own, self.others, self.start, self.count = own, others, start, count
        self.z_only = z_only

    def window(self, core, q, half):
        n = self.count if self.z_only else self.count // 4
        rows = pl.ds(self.start if self.z_only else pl.multiple_of(self.start + q * n, 16), n)
        at, width = core * (D // 2), D // 2
        if half is not None:
            cut = (width // 128 + 1) // 2 * 128
            at, width = (at, cut) if half == 0 else (at + cut, width - cut)
        return rows, pl.ds(pl.multiple_of(at, 128), width)

    def mine(self, core, q):
        return self.own.at[self.window(core, q, None)]

    def one(self, d, core, q, half=None):
        return self.others.at[(d,) + self.window(core, q, half)]

    def all(self, core, q, half=None):
        return self.others.at[(pl.ds(1, 3),) + self.window(core, q, half)]


class Gather:
    def __init__(self, chunks, send):
        core, seq, z, y, x = places()
        p = jnp.where(core == 0, x, y)

        def at(k):
            q = (p + k) % 4
            return (core, jnp.where(core == 0, y * 4 + q, q * 4 + x), z)

        self.core, self.p, self.send, self.chunks = core, p, send, chunks
        self.up, self.down = (core, seq, (z + 1) % 4), (core, seq, (z + 3) % 4)
        self.right, self.left, self.other = at(1), at(3), (1 - core, seq, z)
        self.segments = [
            [(int(op[0]), CHUNKS.index(op[1:])) for op in part.split()] for part in PLAN
        ]
        self.state = [{} for _ in chunks]

    def q(self, k):
        return (self.p + k) % 4

    def along(self, i, k, half, peer):
        part = self.chunks[i].all(self.core, self.q(k), half)
        return self.send(part, part, peer)

    def stage0(self, i):
        c = self.chunks[i]
        mine = c.mine(self.core, self.p)
        self.state[i]["z"] = (
            self.send(mine, c.one(1, self.core, self.p), self.down),
            self.send(mine, c.one(3, self.core, self.p), self.up),
        )

    def stage1(self, i):
        c, st = self.chunks[i], self.state[i]
        core, p = self.core, self.p
        st["z"][0].wait_recv()
        low = self.send(c.one(1, core, p, 0), c.one(2, core, p, 0), self.down)
        st["z"][1].wait_recv()
        high = self.send(c.one(3, core, p, 1), c.one(2, core, p, 1), self.up)
        st["far"] = (low, high)

    def stage2(self, i):
        st = self.state[i]
        for copy in st["far"]:
            copy.wait_recv()
        if self.chunks[i].z_only:
            st["last"] = [self.along(i, 0, None, self.other)]
            return
        st["ring"] = (self.along(i, 0, None, self.right), self.along(i, 0, None, self.left))
        st["last"] = [self.along(i, 0, None, self.other)]

    def stage3(self, i):
        st = self.state[i]
        st["ring"][0].wait_recv()
        low = self.along(i, 3, 0, self.right)
        st["last"].append(self.along(i, 3, None, self.other))
        st["ring"][1].wait_recv()
        high = self.along(i, 1, 1, self.left)
        st["last"].append(self.along(i, 1, None, self.other))
        st["ends"] = (low, high)

    def stage4(self, i):
        st = self.state[i]
        for copy in st["ends"]:
            copy.wait_recv()
        st["last"].append(self.along(i, 2, None, self.other))

    def run(self, op):
        stages = (self.stage0, self.stage1, self.stage2, self.stage3, self.stage4)
        if op[0] <= 2 or not self.chunks[op[1]].z_only:
            stages[op[0]](op[1])

    def step(self):
        for op in self.segments.pop(0) if self.segments else ():
            self.run(op)

    def need(self, i):
        while any(at == i for part in self.segments for _, at in part):
            self.step()
        for copy in self.state[i].pop("last", ()):
            copy.wait_recv()

    def end(self):
        while self.segments:
            self.step()
        for i in range(len(self.chunks)):
            self.need(i)


def position_of(sigma):
    return sigma % 64 // 4 * 16 + sigma // 64 * 4 + sigma % 4


def row_order(to_positions):
    a = lax.broadcasted_iota(jnp.int32, (ROWS, ROWS), 0)
    b = lax.broadcasted_iota(jnp.int32, (ROWS, ROWS), 1)
    hit = (position_of(b) == a) if to_positions else (position_of(a) == b)
    return hit.astype(F32).astype(BF)


def normed(values, gain):
    wide = values.astype(F32)
    scale = lax.rsqrt(jnp.mean(wide * wide, axis=-1, keepdims=True) + NORM_EPS)
    return (wide * scale * gain).astype(BF)


def build_spread(spread):
    r = lax.broadcasted_iota(jnp.int32, (128, 256), 0)
    f = lax.broadcasted_iota(jnp.int32, (128, 256), 1)
    i, j = f % 16, (f + f // 16) % 16
    for h in range(QHEADS):
        for side in range(2):
            base = side * 64 + h * 16
            one = (r == base + i) & (f < 160)
            two = (r == base + j) & (f < 144)
            spread[side, 0, :, 256 * h : 256 * (h + 1)] = one.astype(F32).astype(BF)
            spread[side, 1, :, 256 * h : 256 * (h + 1)] = two.astype(F32).astype(BF)


def features(rows, spread, side):
    f = lax.broadcasted_iota(jnp.int32, (1, 256 * QHEADS), 1) % 256
    one = dot(rows, spread[side, 0]) + (f == 160).astype(F32)
    two = dot(rows, spread[side, 1]) + ((f >= 144) & (f <= 160)).astype(F32)
    return one * two


def key_weights():
    f = lax.broadcasted_iota(jnp.int32, (1, 256 * QHEADS), 1) % 256
    pair = jnp.where((f < 16) | (f >= 128), 1.0 / 32, 1.0 / 16)
    return jnp.where(f < 144, pair, jnp.where(f < 160, 0.25, 1.0)).astype(F32)


def local_layer_one(d, x_normed, w_feat, w_val, unpack, spread, nd, phi, state):
    both = dot(x_normed, w_feat, ((1,), (1,))).astype(BF)
    queries, keys = both[:, :64], both[:, 64:]
    wide = dot(dot(x_normed, w_val, ((1,), (1,))).astype(BF), unpack).astype(BF)
    lane = lax.broadcasted_iota(jnp.int32, (ROWS, 64), 1)
    a = lax.broadcasted_iota(jnp.int32, (ROWS, ROWS), 0)
    b = lax.broadcasted_iota(jnp.int32, (ROWS, ROWS), 1)
    ones = (lax.broadcasted_iota(jnp.int32, (ROWS, 128), 1) == HEAD).astype(F32).astype(BF)
    values = [wide[:, 128 * h : 128 * (h + 1)] + ones for h in range(QHEADS)]
    kernels = []
    for h in range(QHEADS):
        mine = jnp.where(lane // 16 == h, queries, jnp.zeros_like(queries))
        s = dot(mine, keys, ((1,), (1,))) * 0.25
        kernels.append(jnp.where(b <= a, 1.0 + s + 0.5 * s * s, 0.0).astype(BF))
    key_phi = (features(both, spread, 1) * key_weights()).astype(BF)
    phi[d] = features(both, spread, 0).astype(BF)
    for h in range(QHEADS):
        cols = slice(256 * h, 256 * (h + 1))
        state[d * QHEADS + h] = dot(key_phi[:, cols], values[h], ((0,), (0,)))[:STATE].astype(BF)
    for h in range(QHEADS):
        nd[d, :, 128 * h : 128 * (h + 1)] = dot(kernels[h], values[h])


def mix_heads(d, nd, phi, prior, wide):
    full = [
        nd[d, :, 128 * h : 128 * (h + 1)]
        + dot(phi[d, :, 256 * h : 256 * h + STATE], prior[d * QHEADS + h])
        for h in range(QHEADS)
    ]
    for h in range(QHEADS):
        wide[:, 128 * h : 128 * (h + 1)] = (full[h] / full[h][:, HEAD : HEAD + 1]).astype(BF)


def pack_heads():
    a = lax.broadcasted_iota(jnp.int32, (512, 448), 0)
    b = lax.broadcasted_iota(jnp.int32, (512, 448), 1)
    hit = (a // 128 == b // HEAD) & (a % 128 == b % HEAD)
    return hit.astype(F32).astype(BF)


def unpack_heads():
    a = lax.broadcasted_iota(jnp.int32, (448, 512), 0)
    b = lax.broadcasted_iota(jnp.int32, (448, 512), 1)
    hit = (b // 128 == a // HEAD) & (b % 128 == a % HEAD)
    return hit.astype(F32).astype(BF)


def layer_two_part(xn, weight, taps, part, unpack):
    projected = dot(xn, weight[448 * part : 448 * (part + 1)], ((1,), (1,)))
    conv = taps[0, part : part + 1] * projected[HALO - WINDOW :]
    for j in (1, 2):
        conv = conv + taps[j, part : part + 1] * projected[HALO - WINDOW - j : HALO + ROWS - j]
    return dot(conv.astype(BF), unpack).astype(BF)


def attend(first_block, qkv, wide):
    q_at = lax.broadcasted_iota(jnp.int32, (64, 128), 0)
    k_at = lax.broadcasted_iota(jnp.int32, (64, 128), 1) - WINDOW
    band = (k_at <= q_at) & (k_at > q_at - WINDOW)
    inside = band & ((k_at >= 0) | jnp.logical_not(first_block))
    tiles = [(h, 64 * t) for h in range(QHEADS) for t in range(4)]
    logits = []
    for h, at in tiles:
        lanes = slice(128 * h, 128 * (h + 1))
        q = qkv[0, WINDOW + at : WINDOW + at + 64, lanes]
        k = qkv[1, at : at + 128, lanes]
        scaled = dot(q, k, ((1,), (1,))) * HEAD ** (-0.5)
        logits.append(jnp.where(band if at else inside, scaled, -jnp.inf))
    logits = jnp.concatenate(logits, axis=0)
    weights = jnp.exp(logits - jnp.max(logits, axis=1, keepdims=True))
    attention = (weights / jnp.sum(weights, axis=1, keepdims=True)).astype(BF)
    for n, (h, at) in enumerate(tiles):
        lanes = slice(128 * h, 128 * (h + 1))
        v = qkv[2, at : at + 128, lanes]
        wide[at : at + 64, lanes] = dot(attention[64 * n : 64 * (n + 1)], v).astype(BF)


def layers_kernel(
    live, wanted, gain, gain_two, outgoing, feat, val, out_one, win, out_two, taps,
    out,
    w_feat, w_val, w_out, w_win, w_two, w_taps, pages, tokens, arrived, spread, xn, nd, phi,
    state, blocks, prefix, prior, wide, total, residual, halo, qkv, ends,
    send_sems, recv_sems, local_sems, page_sems, token_sems, state_sems, prior_sems, halo_sems, out_sems,
):
    core, seq, z, _, _ = places()
    place = core * 16 + seq
    send = Sender(send_sems, recv_sems)
    chunks = [
        Chunk(feat, w_feat, 0, 128),
        Chunk(val, w_val, 0, 192),
        Chunk(val, w_val, 192, 256),
        Chunk(out_one, w_out, 0, 448),
        Chunk(win, w_win, 0, 448),
        Chunk(win, w_win, 448, 448),
        Chunk(win, w_win, 896, 448),
        Chunk(out_two, w_two, 0, 448, True),
    ]
    gather = Gather(chunks, send)
    first_block = seq == 0

    def copy_to(src, dst, sems, k, peer):
        return pltpu.make_async_remote_copy(
            src_ref=src, dst_ref=dst, send_sem=sems.at[0, k], recv_sem=sems.at[1, k],
            device_id=peer, device_id_type=MESH,
        )

    own = [
        pltpu.make_async_copy(feat, w_feat.at[0], local_sems.at[0]),
        pltpu.make_async_copy(val, w_val.at[0], local_sems.at[1]),
        pltpu.make_async_copy(out_one, w_out.at[0], local_sems.at[2]),
        pltpu.make_async_copy(outgoing.at[place], pages.at[place], local_sems.at[3]),
        pltpu.make_async_copy(win, w_win.at[0], local_sems.at[4]),
        pltpu.make_async_copy(out_two, w_two.at[0], local_sems.at[5]),
        pltpu.make_async_copy(taps, w_taps.at[0], local_sems.at[6]),
    ]
    barrier = pltpu.get_barrier_semaphore()
    plane = [((place + k) % 32 // 16, (place + k) % 16, z) for k in range(1, 32)]
    greeted = [(core, seq, (z + k) % 4) for k in (1, 2, 3)] + plane
    for peer in greeted:
        pl.semaphore_signal(barrier, inc=1, device_id=peer, device_id_type=MESH)
    for copy in own:
        copy.start()
    build_spread(spread)
    pl.semaphore_wait(barrier, len(greeted))
    page_copies = [
        copy_to(outgoing.at[(place + k) % 32], pages.at[place], page_sems, k, plane[k - 1])
        for k in range(1, 32)
    ]
    for copy in page_copies:
        copy.start()
    gather.step()
    own[3].wait()
    for copy in page_copies:
        copy.wait_recv()
    column = lax.broadcasted_iota(jnp.int32, (ROWS, ROWS), 1)
    chosen = (wanted[...] == column).astype(F32).astype(BF)
    rows = pages[...].astype(F32).reshape(ROWS, D).astype(BF)
    tokens[...] = dot(chosen, rows).astype(BF).reshape(QUARTERS, 64, D)
    kept = pltpu.make_async_copy(tokens.at[z], arrived.at[z], local_sems.at[3])
    kept.start()
    token_copies = [
        copy_to(tokens.at[(z + k) % 4], arrived.at[z], token_sems, k, (core, seq, (z + k) % 4))
        for k in (1, 2, 3)
    ]
    for copy in token_copies:
        copy.start()
    small = [send(taps, w_taps.at[d], (core, seq, (z + 4 - d) % 4)) for d in (1, 2, 3)]
    gather.step()
    kept.wait()
    for copy in token_copies:
        copy.wait_recv()
    residual[...] = dot(row_order(True), arrived[...].reshape(ROWS, D)).astype(BF)
    xn[HALO:] = normed(residual[...], gain[...].reshape(1, D))
    gather.step()
    own[0].wait()
    own[1].wait()
    unpack = unpack_heads()

    def state_copy(head, sender):
        return pltpu.make_async_remote_copy(
            src_ref=state.at[head], dst_ref=blocks.at[sender], send_sem=state_sems.at[0, head],
            recv_sem=state_sems.at[1, sender], device_id=(core, head, z), device_id_type=MESH,
        )

    def prior_copy(block, head):
        return pltpu.make_async_remote_copy(
            src_ref=prefix.at[block], dst_ref=prior.at[head], send_sem=prior_sems.at[0, block],
            recv_sem=prior_sems.at[1, head], device_id=(core, block, z), device_id_type=MESH,
        )

    def add_up():
        kept = pltpu.make_async_copy(state.at[seq], blocks.at[seq], local_sems.at[3])
        kept.start()
        kept.wait()
        for k in range(1, 16):
            state_copy(seq, (seq + k) % 16).wait_recv()
        prefix[0] = jnp.zeros((STATE, 128), BF)

        def add(b, before):
            now = before + blocks[b].astype(F32)
            prefix[b + 1] = now.astype(BF)
            return now

        lax.fori_loop(0, 15, add, jnp.zeros((STATE, 128), F32))
        for k in range(1, 16):
            prior_copy((seq + k) % 16, seq).start()
        kept = pltpu.make_async_copy(prefix.at[seq], prior.at[seq], local_sems.at[3])
        kept.start()
        kept.wait()

    for d in range(QUARTERS):
        if d == 1:
            for i in range(3):
                gather.need(i)
        local_layer_one(d, xn[HALO:], w_feat[d], w_val[d], unpack, spread, nd, phi, state)
        for head in range(d * QHEADS, (d + 1) * QHEADS):

            @pl.when(seq != head)
            def _():
                state_copy(head, seq).start()

        gather.step()
        if d >= 1:
            pl.when(seq // QHEADS == d - 1)(add_up)
    gather.step()
    pl.when(seq // QHEADS == QUARTERS - 1)(add_up)
    gather.step()
    pack = pack_heads()
    own[2].wait()
    for d in range(QUARTERS):
        for head in range(d * QHEADS, (d + 1) * QHEADS):

            @pl.when(seq != head)
            def _():
                prior_copy(seq, head).wait_recv()

        mix_heads(d, nd, phi, prior, wide)
        mixed = dot(wide[...], pack).astype(BF)
        if d == 1:
            gather.need(3)
        part = dot(mixed, w_out[d]).astype(BF).astype(F32)
        total[...] = part if d == 0 else total[...] + part
        gather.step()
    residual[...] = (residual[...].astype(F32) + total[...]).astype(BF)
    hand_on = copy_to(
        residual.at[pl.ds(ROWS - HALO, HALO)], halo, halo_sems, 0, (core, (seq + 1) % 16, z)
    )
    hand_on.start()
    xn[HALO:] = normed(residual[...], gain_two[...].reshape(1, D))
    gather.step()
    hand_on.wait_recv()
    before = halo[...]
    xn[:HALO] = normed(jnp.where(first_block, jnp.zeros_like(before), before), gain_two[...].reshape(1, D))
    for copy in own[4:]:
        copy.wait()
    for copy in small:
        copy.wait_recv()
    for part in range(3):
        for d in range(QUARTERS):
            if d == 1:
                gather.need(4 + part)
            qkv[d, part] = layer_two_part(xn[...], w_win.at[d], w_taps.at[d], part, unpack)
        gather.step()
    for d in range(QUARTERS):
        attend(first_block, qkv.at[d], wide)
        mixed = dot(wide[...], pack).astype(BF)
        if d == 1:
            gather.end()
        part = dot(mixed, w_two[d]).astype(BF).astype(F32)
        total[...] = part if d == 0 else total[...] + part
    row = lax.broadcasted_iota(jnp.int32, (ROWS, 1), 0) + seq * ROWS
    result = (residual[...].astype(F32) + total[...]).astype(BF)
    result = jnp.where(row < live[core * 4 + z], result, jnp.zeros_like(result))
    for copy in token_copies:
        copy.wait_send()
    ends[...] = dot(row_order(False), result).reshape(QUARTERS, 16, 4, D).astype(BF)
    kept = pltpu.make_async_copy(ends.at[z], out.at[z], local_sems.at[3])
    kept.start()
    finals = [
        copy_to(ends.at[(z + k) % 4], out.at[z], out_sems, k, (core, seq, (z + k) % 4))
        for k in (2, 1, 3)
    ]
    for copy in finals:
        copy.start()
    kept.wait()
    for copy in finals:
        copy.wait()
    hand_on.wait_send()
    for k in range(1, 16):
        prior_copy((seq + k) % 16, seq).wait_send()
    for copy in page_copies + send.copies:
        copy.wait_send()
    for head in range(16):

        @pl.when(seq != head)
        def _():
            state_copy(head, seq).wait_send()


def layers(live, *arrays):
    heads = QUARTERS * QHEADS
    bulk = 7 * 12 + 5 + 3
    dma = pltpu.SemaphoreType.DMA
    return pl.pallas_call(
        layers_kernel,
        out_shape=jax.ShapeDtypeStruct((QUARTERS, 16, 4, D), BF),
        in_specs=[pl.BlockSpec(memory_space=pltpu.SMEM)] + [VM] * 3 + [ANY] * 7,
        out_specs=ANY,
        scratch_shapes=[
            pltpu.VMEM((QUARTERS, 128, D), BF),
            pltpu.VMEM((QUARTERS, 448, D), BF),
            pltpu.VMEM((QUARTERS, 448, D), BF),
            pltpu.VMEM((QUARTERS, 1344, D), BF),
            pltpu.VMEM((QUARTERS, 448, D), BF),
            pltpu.VMEM((QUARTERS, 3, 3, 448), F32),
            pltpu.VMEM((32, 8, D), BF),
            pltpu.VMEM((QUARTERS, 64, D), BF),
            pltpu.VMEM((QUARTERS, 64, D), BF),
            pltpu.VMEM((2, 2, 128, 256 * QHEADS), BF),
            pltpu.VMEM((ROWS + HALO, D), BF),
            pltpu.VMEM((QUARTERS, ROWS, 512), F32),
            pltpu.VMEM((QUARTERS, ROWS, 1024), BF),
            pltpu.VMEM((heads, STATE, 128), BF),
            pltpu.VMEM((16, STATE, 128), BF),
            pltpu.VMEM((16, STATE, 128), BF),
            pltpu.VMEM((heads, STATE, 128), BF),
            pltpu.VMEM((ROWS, 512), BF),
            pltpu.VMEM((ROWS, D), F32),
            pltpu.VMEM((ROWS, D), BF),
            pltpu.VMEM((HALO, D), BF),
            pltpu.VMEM((QUARTERS, 3, ROWS + WINDOW, 512), BF),
            pltpu.VMEM((QUARTERS, 16, 4, D), BF),
            dma((bulk,)),
            dma((bulk,)),
            dma((7,)),
            dma((2, 32)),
            dma((2, 4)),
            dma((2, 16)),
            dma((2, 16)),
            dma((2, 1)),
            dma((2, 4)),
        ],
        compiler_params=pltpu.CompilerParams(
            collective_id=0, has_side_effects=True, vmem_limit_bytes=63 << 20
        ),
        name="layers",
    )(live, *arrays)


def on_device(
    pool, page_table, reassign, lengths, gain_one, w_featmap, w_value, w_out_one,
    gain_two, w_window, conv_window, w_out_two,
):
    groups = 32
    device_place = lax.axis_index(("dp", "seq"))
    seq, core, z = lax.axis_index("seq"), lax.axis_index("dp"), lax.axis_index("tensor")
    pages_dev, page_share = pool.shape[:2]
    table = page_table[reassign]
    source = table.reshape(2, 4, 16, 16).transpose(0, 2, 1, 3).reshape(groups, pages_dev)
    owner, slot_of = source // pages_dev, source % pages_dev
    before = jnp.arange(pages_dev)[None, :] < jnp.arange(pages_dev)[:, None]
    rank = jnp.sum((owner[:, :, None] == owner[:, None, :]) & before[None], axis=2)
    hit = (owner == device_place)[:, None, :] & (rank[:, None, :] == jnp.arange(2)[None, :, None])
    send_slot = jnp.sum(jnp.where(hit, slot_of[:, None, :], 0), axis=2)
    outgoing = jnp.take(pool, send_slot.reshape(-1), axis=0).reshape(groups, 8, D)
    row_hit = (jnp.arange(groups) == device_place)[:, None]
    pick = jnp.sum(jnp.where(row_hit, owner * 2 + rank, 0), axis=0)
    wanted = (pick[:, None] * 4 + jnp.arange(4)[None, :]).reshape(ROWS, 1)
    feat = w_featmap.transpose(1, 2, 0).reshape(128, D)
    win = w_window.transpose(1, 2, 0).reshape(1344, D)
    result = layers(
        lengths[reassign], wanted, gain_one, gain_two, outgoing, feat, w_value.T,
        w_out_one, win, w_out_two, conv_window,
    )
    return result


def solution(mesh):
    return jax.shard_map(
        on_device,
        mesh=mesh,
        in_specs=(
            P(("dp", "seq"), "tensor", None),
            P(),
            P(),
            P(),
            P(),
            P(None, None, "tensor"),
            P(None, "tensor"),
            P("tensor", None),
            P(),
            P(None, None, "tensor"),
            P(None, None, "tensor"),
            P("tensor", None),
        ),
        out_specs=P("dp", "seq", "tensor", None),
        check_vma=False,
    )
```
